32 devices in a mesh: dp: 8 (over z, y), ctx: 4 (over x, core).
Axes of the slice: x: 2, y: 2, z: 4, core: 2. Of those that a mesh axis runs over, the one named last changes fastest.
Arguments:
- tokens: bfloat16 [8, 1024, 4096], P('dp', 'ctx'), may hold values from -7 to 7
- block_order: int32 [8, 8], P('dp', 'ctx'), may hold values from 0 to 7, as said below
- doc_ids: int32 [8, 1024], P('dp', 'ctx'), may hold values from 0 to 1, as said below
- w_qkv: bfloat16 [4096, 768], P('dp'), as said below
- grad_out: bfloat16 [8, 1024, 512], P('dp', 'ctx'), may hold values from -6 to 6
Outputs:
- attended: bfloat16 [8, 1024, 512], P('dp', 'ctx')
- grad_tokens: bfloat16 [8, 1024, 4096], P('dp', 'ctx')
- grad_w: float32 [4096, 768], P(('dp', 'ctx'))
The draws below stay inside these ranges and needn't reach their ends.
Inputs may be any that keep to these rules, and one draw needn't show every extreme that they name: `block_order`: each row holds every block number of its sequence once; stored blocks 2 r and 2 r + 1 hold numbers that sum to 7. `doc_ids`: taken in order of sequence position, a sequence's document numbers start at 0, never fall and rise by at most one; every sequence reaches the largest number. `w_qkv`: entries lie within 4 / sqrt(4096) of zero.
All inputs are finite; a program needn't handle non-finite values.
Results may differ from the reference program's by a relative error of at most 0.02.
Values may be sent and summed in bfloat16 or wider, within the bound.
No kernel may reach another device: no remote copies, remote signals or barrier semaphores. Data moves between devices by JAX's collectives and lax.ppermute only.
A program may use at most 128 MiB of HBM per device.

```python
import math
import jax
import jax.numpy as jnp
from jax import lax

D = 4096
HQ = 4
HD = 128
BLOCK = 128
SEQ = 1024
BATCH = 8


def layout_draw(key):
    block_count = SEQ // BLOCK
    doc_count = SEQ // (4 * BLOCK)

    def one_sequence(index):
        seeded = jax.random.fold_in(jax.random.fold_in(key, 11), index)
        key_pairs, key_flip, key_docs = jax.random.split(seeded, 3)
        pairs = jax.random.permutation(key_pairs, block_count // 2)
        flips = jax.random.randint(key_flip, (block_count // 2,), 0, 2)
        lower = jnp.where(flips == 1, block_count - 1 - pairs, pairs)
        upper = block_count - 1 - lower
        order = jnp.stack([lower, upper], axis=1).reshape(block_count).astype(jnp.int32)
        cuts = jax.random.permutation(key_docs, SEQ - 1)[:doc_count - 1].astype(jnp.int32) + 1
        flags = jnp.zeros((SEQ,), jnp.int32).at[cuts].set(1)
        natural = jnp.cumsum(flags).astype(jnp.int32)
        positions = (order[:, None] * BLOCK + jnp.arange(BLOCK, dtype=jnp.int32)).reshape(SEQ)
        return (order, natural[positions].astype(jnp.int32))
    return jax.vmap(one_sequence)(jnp.arange(BATCH))


def draw_block_order(key, part):
    return layout_draw(key)[0]


def draw_doc_ids(key, part):
    return layout_draw(key)[1]


def draw_tokens(key, part):
    shape = (BATCH, SEQ, D)
    values = jnp.clip(jax.random.normal(key, shape, jnp.float32), -6.0, 6.0)
    return values.astype(jnp.bfloat16)


def draw_w_qkv(key, part):
    column_count = (HQ + 2) * HD
    limit = 4.0 / math.sqrt(D)
    mixed = jax.random.normal(key, (D, column_count), jnp.float32) / math.sqrt(D)
    return jnp.clip(mixed, -limit, limit).astype(jnp.bfloat16)


def level_of(own_key, shape, cuts, smallest, top_value):
    gain = 1.0
    for axis_at, blocks in cuts:
        heights = jax.random.uniform(jax.random.fold_in(jax.random.fold_in(own_key, 6), axis_at), (blocks,), jnp.float32, smallest / len(cuts), top_value / len(cuts))
        gain = gain * jnp.repeat(jnp.exp(heights), shape[axis_at] // blocks).reshape((-1,) + (1,) * (len(shape) - 1 - axis_at))
    return gain


def scatter_about(rng, extent, width, bound, cuts=(), kind=jnp.bfloat16):
    loudness = level_of(rng, extent, cuts, -0.22, 0.18) if cuts else 1.0
    result = jax.random.normal(rng, extent, jnp.float32) * width * loudness
    return jnp.minimum(jnp.maximum(result, -bound), bound).astype(kind)


def setup_inputs(seed: int = 0) -> dict:
    splits = jax.random.split(jax.random.key(seed), 6)
    return {
        "tokens": draw_tokens(jax.random.fold_in(splits[5], 71), 0),
        "block_order": draw_block_order(jax.random.fold_in(splits[5], 71), 0),
        "doc_ids": draw_doc_ids(jax.random.fold_in(splits[5], 71), 0),
        "w_qkv": draw_w_qkv(jax.random.fold_in(splits[5], 71), 0),
        "grad_out": scatter_about(splits[4], (BATCH, SEQ, HQ * HD), 1.0, 6.0, ((0, 8), (1, 4))),
    }


ROPE_BASE = 500000.0

def token_positions(order):
    within = jnp.arange(BLOCK, dtype=jnp.int32)
    spread = order[..., :, None] * BLOCK + within
    return spread.reshape(order.shape[:-1] + (order.shape[-1] * BLOCK,)).astype(jnp.int32)

def rope_tables(positions, head_size):
    half_size = head_size // 2
    inverse = 1.0 / ROPE_BASE ** (jnp.arange(half_size, dtype=jnp.float32) * (2.0 / head_size))
    angles = positions.astype(jnp.float32)[..., None] * inverse
    return (jnp.cos(angles), jnp.sin(angles))

def rotate(values, cosine_table, sine_table):
    half_size = values.shape[-1] // 2
    leading = values[..., :half_size]
    trailing = values[..., half_size:]
    return jnp.concatenate([leading * cosine_table - trailing * sine_table, trailing * cosine_table + leading * sine_table], axis=-1)

def reference(tokens, block_order, doc_ids, w_qkv, grad_out):
    score_scale = 1.0 / math.sqrt(HD)
    width_q = HQ * HD

    def one_sequence(grad_total, packed):
        inputs, order, docs, out_grad = packed
        length = inputs.shape[0]
        positions = token_positions(order)
        projected = jnp.dot(inputs, w_qkv, preferred_element_type=jnp.float32)
        cosine_table, sine_table = rope_tables(positions, HD)
        queries = rotate(projected[:, :width_q].reshape(length, HQ, HD), cosine_table[:, None, :], sine_table[:, None, :]).astype(jnp.bfloat16)
        key_rows = rotate(projected[:, width_q:width_q + HD], cosine_table, sine_table).astype(jnp.bfloat16)
        value_rows = projected[:, width_q + HD:].astype(jnp.bfloat16)
        allowed = (docs[:, None] == docs[None, :]) & (positions[None, :] <= positions[:, None])

        def head_pass(head_args):
            query_head, grad_head = head_args
            scores = jnp.dot(query_head, key_rows.T, preferred_element_type=jnp.float32) * score_scale
            row_max = lax.optimization_barrier(jnp.max(jnp.where(allowed, scores, -jnp.inf), axis=1))
            shifted = jnp.where(allowed, jnp.exp(scores - row_max[:, None]), 0.0)
            row_sum = lax.optimization_barrier(jnp.sum(shifted, axis=1))
            attended = (jnp.dot(shifted.astype(jnp.bfloat16), value_rows, preferred_element_type=jnp.float32) / row_sum[:, None]).astype(jnp.bfloat16)
            log_norm = row_max + jnp.log(row_sum)
            row_dots = lax.optimization_barrier(jnp.sum(grad_head.astype(jnp.float32) * attended.astype(jnp.float32), axis=1))
            chances = jnp.where(allowed, jnp.exp(scores - log_norm[:, None]), 0.0)
            lowered = chances.astype(jnp.bfloat16)
            value_grad = jnp.dot(lowered.T, grad_head, preferred_element_type=jnp.float32)
            prob_grad = jnp.dot(grad_head, value_rows.T, preferred_element_type=jnp.float32)
            score_grad = (chances * (prob_grad - row_dots[:, None])).astype(jnp.bfloat16)
            query_grad = jnp.dot(score_grad, key_rows, preferred_element_type=jnp.float32) * score_scale
            key_grad = jnp.dot(score_grad.T, query_head, preferred_element_type=jnp.float32) * score_scale
            return (attended, query_grad, key_grad, value_grad)
        head_queries = jnp.transpose(queries, (1, 0, 2))
        head_grads = jnp.transpose(out_grad.reshape(length, HQ, HD), (1, 0, 2))
        attended, query_grad, key_grad, value_grad = lax.map(head_pass, (head_queries, head_grads))
        key_grad = lax.optimization_barrier(jnp.sum(key_grad, axis=0))
        value_grad = lax.optimization_barrier(jnp.sum(value_grad, axis=0))
        query_raw = rotate(jnp.transpose(query_grad, (1, 0, 2)), cosine_table[:, None, :], -sine_table[:, None, :])
        key_raw = rotate(key_grad, cosine_table, -sine_table)
        qkv_grad = jnp.concatenate([query_raw.reshape(length, width_q), key_raw, value_grad], axis=1).astype(jnp.bfloat16)
        grad_inputs = jnp.dot(qkv_grad, w_qkv.T, preferred_element_type=jnp.float32).astype(jnp.bfloat16)
        grad_total = grad_total + jnp.dot(inputs.T, qkv_grad, preferred_element_type=jnp.float32)
        attended_flat = jnp.transpose(attended, (1, 0, 2)).reshape(length, width_q)
        return (grad_total, (attended_flat, grad_inputs))
    start_grad = jnp.zeros((w_qkv.shape[0], w_qkv.shape[1]), jnp.float32)
    grad_w, outputs = lax.scan(one_sequence, start_grad, (tokens, block_order, doc_ids, grad_out))
    return (outputs[0], outputs[1], grad_w)
```

```python
import math
from functools import partial

import jax
import jax.numpy as jnp
from jax import lax
from jax.experimental import pallas as pl
from jax.experimental.pallas import tpu as pltpu
from jax.sharding import PartitionSpec as P

HQ = 4
HD = 128
BLOCK = 128
WQ = HQ * HD
ROPE_BASE = 500000.0
NEG_FILL = -1e30
BF16 = jnp.bfloat16
F32 = jnp.float32


def rope_tables(positions):
    half = HD // 2
    inverse = 1.0 / ROPE_BASE ** (jnp.arange(half, dtype=F32) * (2.0 / HD))
    angles = positions.astype(F32)[..., None] * inverse
    return (jnp.cos(angles), jnp.sin(angles))


def rotate(values, cosine_table, sine_table):
    half = values.shape[-1] // 2
    leading = values[..., :half]
    trailing = values[..., half:]
    return jnp.concatenate(
        [
            leading * cosine_table - trailing * sine_table,
            trailing * cosine_table + leading * sine_table,
        ],
        axis=-1,
    )


def flip_bits(array, axis, size, index):
    bit = 1
    while bit < size:
        shape = array.shape
        split = array.reshape(shape[:axis] + (size // (2 * bit), 2, bit) + shape[axis + 1 :])
        array = jnp.where((index & bit) != 0, jnp.flip(split, axis + 1), split).reshape(shape)
        bit *= 2
    return array


def exchange(array, axis, size, offset):
    return lax.ppermute(array, axis, [(i, i ^ offset) for i in range(size)])


def block_kernel(dims, width, scatter, index_ref, in_ref, out_ref):
    n_core, n_x, n_y, n_z = dims
    row, col = index_ref[0], index_ref[1]
    for p in range(n_core * n_x * n_y * n_z):
        jz, rest = p % n_z, p // n_z
        jy, rest = rest % n_y, rest // n_y
        jx, jc = rest % n_x, rest // n_x
        place = (row ^ (jz * n_y + jy)) * (n_x * n_core) + (col ^ (jx * n_core + jc))
        dynamic = pl.ds(pl.multiple_of(place * width, width), width)
        static = pl.ds(p * width, width)
        if scatter:
            out_ref[:, dynamic] = in_ref[:, static]
        else:
            out_ref[:, static] = in_ref[:, dynamic]


def reorder(array, dims, row, col, scatter):
    n_core, n_x, n_y, n_z = dims
    width = array.shape[1] // (n_core * n_x * n_y * n_z)
    if width % 128 == 0:
        return pl.pallas_call(
            partial(block_kernel, dims, width, scatter),
            out_shape=jax.ShapeDtypeStruct(array.shape, array.dtype),
            grid_spec=pltpu.PrefetchScalarGridSpec(
                num_scalar_prefetch=1,
                grid=(1,),
                in_specs=[pl.BlockSpec(array.shape, lambda i, s: (0, 0))],
                out_specs=pl.BlockSpec(array.shape, lambda i, s: (0, 0)),
            ),
            cost_estimate=pl.CostEstimate(
                flops=0, bytes_accessed=4 * array.size, transcendentals=0
            ),
            name="scatter_columns" if scatter else "gather_columns",
        )(jnp.stack([row, col]).astype(jnp.int32), array)
    count = array.shape[0]
    rows, cols = n_y * n_z, n_x * n_core
    if scatter:
        split = array.reshape(count, n_core, n_x, n_y, n_z, width).transpose(0, 4, 3, 2, 1, 5)
    else:
        split = array
    split = split.reshape(count, rows, cols, width)
    split = flip_bits(flip_bits(split, 1, rows, row), 2, cols, col)
    if not scatter:
        split = split.reshape(count, n_z, n_y, n_x, n_core, width).transpose(0, 4, 3, 2, 1, 5)
    return split.reshape(array.shape)


def on_device(n_dp, n_ctx, tokens, block_order, doc_ids, w_qkv, grad_out):
    inputs = tokens[0]
    row_count, features = inputs.shape
    score_scale = 1.0 / math.sqrt(HD)
    n_core, n_x = 2, n_ctx // 2
    n_z = 4
    n_y = n_dp // n_z
    dims = (n_core, n_x, n_y, n_z)
    row, col = lax.axis_index("dp"), lax.axis_index("ctx")
    over_z = lambda a, o: exchange(a, "dp", n_dp, o * n_y)
    over_y = lambda a, o: exchange(a, "dp", n_dp, o)
    over_x = lambda a, o: exchange(a, "ctx", n_ctx, o * n_core)
    over_core = lambda a: exchange(a, "ctx", n_ctx, 1)
    near = lambda n: range(1, n)

    facts = jnp.concatenate([doc_ids[0], block_order[0]])
    facts_x = jnp.stack([facts] + [over_x(facts, o) for o in near(n_x)])
    facts_all = jnp.stack([facts_x, over_core(facts_x)]).reshape(n_ctx, -1)
    docs_all = facts_all[:, :row_count].reshape(-1)
    order_all = facts_all[:, row_count:]
    pos_all = (order_all[:, :, None] * BLOCK + jnp.arange(BLOCK, dtype=jnp.int32)).reshape(-1)
    docs_here, pos_here = docs_all[:row_count], pos_all[:row_count]

    shard = w_qkv.shape[0]
    piece = shard // n_ctx
    own = w_qkv.reshape(n_x * n_core, piece, -1)
    own = flip_bits(own, 0, n_ctx, col).reshape(n_x, n_core, piece, -1)

    def gather_yz(first):
        by_z = jnp.stack([first] + [over_z(first, o) for o in near(n_z)])
        rows = [by_z]
        for o in near(n_y):
            rows.append(jnp.concatenate([over_y(first, o)[None], over_y(by_z[1:], o)]))
        return jnp.stack(rows)

    kv_half = gather_yz(own[:, 0, :, WQ:])
    kv_half = jnp.moveaxis(kv_half, 2, 0)
    kv_half = jnp.stack([kv_half, over_core(kv_half)])
    w_kv = kv_half.reshape(features, 2 * HD)

    q_part = gather_yz(own[0, 0, :, :WQ])
    q_half = jnp.stack([q_part] + [over_x(q_part, o) for o in near(n_x)])
    q_full = jnp.stack([q_half, over_core(q_half)])
    w_q = q_full.reshape(features, WQ)

    near_inputs = reorder(inputs, dims, row, col, False)
    projected_kv = jnp.dot(near_inputs, w_kv, preferred_element_type=F32)
    cosine_table, sine_table = rope_tables(pos_here)
    key_here = rotate(projected_kv[:, :HD], cosine_table, sine_table).astype(BF16)
    value_here = projected_kv[:, HD:].astype(BF16)
    kv_here = jnp.concatenate([key_here, value_here], axis=1)
    kv_x = jnp.stack([kv_here] + [over_x(kv_here, o) for o in near(n_x)])
    kv_core = jnp.concatenate([over_core(kv_here)[None], over_core(kv_x[1:])])
    kv_all = jnp.concatenate([kv_x, kv_core]).reshape(-1, 2 * HD)
    keys, values = kv_all[:, :HD], kv_all[:, HD:]

    projected_q = jnp.dot(near_inputs, w_q, preferred_element_type=F32)
    queries = rotate(
        projected_q.reshape(row_count, HQ, HD),
        cosine_table[:, None, :],
        sine_table[:, None, :],
    ).astype(BF16)

    allowed = (docs_here[:, None] == docs_all[None, :]) & (pos_all[None, :] <= pos_here[:, None])
    allowed = allowed[:, None, :]
    scores = jnp.einsum("thd,nd->thn", queries, keys, preferred_element_type=F32) * score_scale
    row_max = jnp.max(jnp.where(allowed, scores, NEG_FILL), axis=-1)
    shifted = jnp.where(allowed, jnp.exp(scores - row_max[..., None]), 0.0)
    row_sum = jnp.sum(shifted, axis=-1)
    weighted = jnp.einsum("thn,nd->thd", shifted.astype(BF16), values, preferred_element_type=F32)
    attended = (weighted / row_sum[..., None]).astype(BF16)
    log_norm = row_max + jnp.log(row_sum)
    out_grad = grad_out[0].reshape(row_count, HQ, HD)
    row_dots = jnp.sum(out_grad.astype(F32) * attended.astype(F32), axis=-1)
    chances = jnp.where(allowed, jnp.exp(scores - log_norm[..., None]), 0.0)
    value_term = jnp.einsum(
        "thn,thd->nd", chances.astype(BF16), out_grad, preferred_element_type=F32
    )
    prob_grad = jnp.einsum("thd,nd->thn", out_grad, values, preferred_element_type=F32)
    score_grad = (chances * (prob_grad - row_dots[..., None])).astype(BF16)
    query_grad = (
        jnp.einsum("thn,nd->thd", score_grad, keys, preferred_element_type=F32) * score_scale
    )
    key_term = (
        jnp.einsum("thn,thd->nd", score_grad, queries, preferred_element_type=F32) * score_scale
    )
    kv_terms = jnp.concatenate([key_term, value_term], axis=1)
    kv_terms = kv_terms.reshape(n_core, n_x, row_count, 2 * HD)
    kv_sum = kv_terms[0] + over_core(kv_terms[1].astype(BF16)).astype(F32)
    kv_send = kv_sum[1:].astype(BF16)
    kv_mine = kv_sum[0]
    for o in near(n_x):
        kv_mine = kv_mine + over_x(kv_send[o - 1], o).astype(F32)

    q_grad = rotate(query_grad, cosine_table[:, None, :], -sine_table[:, None, :])
    q_grad = q_grad.reshape(row_count, WQ).astype(BF16)
    key_raw = rotate(kv_mine[:, :HD], cosine_table, -sine_table)
    kv_grad = jnp.concatenate([key_raw, kv_mine[:, HD:]], axis=1).astype(BF16)

    def weight_terms(columns, grad):
        return lax.dot_general(
            columns, grad, (((0,), (0,)), ((), ())), preferred_element_type=F32
        )

    half = features // 2

    def core_sum(grad):
        sent = over_core(weight_terms(near_inputs[:, half:], grad).astype(BF16))
        kept = weight_terms(near_inputs[:, :half], grad) + sent.astype(F32)
        return kept.reshape(n_x, n_y, n_z, piece, -1)

    def reduce_first(terms, over):
        total = terms[0]
        for o in near(terms.shape[0]):
            total = total + over(terms[o].astype(BF16), o).astype(F32)
        return total

    q_terms = core_sum(q_grad)
    q_terms = reduce_first(q_terms, over_x)
    q_terms = reduce_first(q_terms, over_y)
    q_terms = reduce_first(q_terms, over_z)

    kv_sums = core_sum(kv_grad)
    kv_sums = reduce_first(jnp.moveaxis(kv_sums, 0, 2), over_y)
    kv_sums = reduce_first(kv_sums, over_z)
    kv_sums = reduce_first(kv_sums, over_x)
    grad_w = jnp.concatenate([q_terms, kv_sums], axis=1)

    near_grad = (
        lax.dot_general(q_grad, w_q, (((1,), (1,)), ((), ())), preferred_element_type=F32)
        + lax.dot_general(kv_grad, w_kv, (((1,), (1,)), ((), ())), preferred_element_type=F32)
    ).astype(BF16)
    grad_inputs = reorder(near_grad, dims, row, col, True)
    return (attended.reshape(1, row_count, WQ), grad_inputs[None], grad_w)


def solution(mesh):
    in_specs = (
        P("dp", "ctx", None),
        P("dp", "ctx"),
        P("dp", "ctx"),
        P("dp", None),
        P("dp", "ctx", None),
    )
    out_specs = (P("dp", "ctx", None), P("dp", "ctx", None), P(("dp", "ctx"), None))
    return jax.shard_map(
        partial(on_device, mesh.shape["dp"], mesh.shape["ctx"]),
        mesh=mesh,
        in_specs=in_specs,
        out_specs=out_specs,
        check_vma=False,
    )
```

```python
import math
from functools import partial

import jax
import jax.numpy as jnp
from jax import lax
from jax.experimental import pallas as pl
from jax.experimental.pallas import tpu as pltpu
from jax.sharding import PartitionSpec as P

HQ = 4
HD = 128
BLOCK = 128
WQ = HQ * HD
ROPE_BASE = 500000.0
NEG_FILL = -1e30
BF16 = jnp.bfloat16
F32 = jnp.float32


def rope_tables(positions):
    half = HD // 2
    inverse = 1.0 / ROPE_BASE ** (jnp.arange(half, dtype=F32) * (2.0 / HD))
    angles = positions.astype(F32)[..., None] * inverse
    return (jnp.cos(angles), jnp.sin(angles))


def rotate(values, cosine_table, sine_table):
    half = values.shape[-1] // 2
    leading = values[..., :half]
    trailing = values[..., half:]
    return jnp.concatenate(
        [
            leading * cosine_table - trailing * sine_table,
            trailing * cosine_table + leading * sine_table,
        ],
        axis=-1,
    )


def flip_bits(array, axis, size, index):
    bit = 1
    while bit < size:
        shape = array.shape
        split = array.reshape(shape[:axis] + (size // (2 * bit), 2, bit) + shape[axis + 1 :])
        array = jnp.where((index & bit) != 0, jnp.flip(split, axis + 1), split).reshape(shape)
        bit *= 2
    return array


def exchange(array, axis, size, offset):
    return lax.ppermute(array, axis, [(i, i ^ offset) for i in range(size)])


def block_kernel(dims, width, scatter, index_ref, in_ref, out_ref):
    n_core, n_x, n_y, n_z = dims
    row, col = index_ref[0], index_ref[1]
    for p in range(n_core * n_x * n_y * n_z):
        jz, rest = p % n_z, p // n_z
        jy, rest = rest % n_y, rest // n_y
        jx, jc = rest % n_x, rest // n_x
        place = (row ^ (jz * n_y + jy)) * (n_x * n_core) + (col ^ (jx * n_core + jc))
        dynamic = pl.ds(pl.multiple_of(place * width, width), width)
        static = pl.ds(p * width, width)
        if scatter:
            out_ref[:, dynamic] = in_ref[:, static]
        else:
            out_ref[:, static] = in_ref[:, dynamic]


def reorder(array, dims, row, col, scatter):
    n_core, n_x, n_y, n_z = dims
    width = array.shape[1] // (n_core * n_x * n_y * n_z)
    if width % 128 == 0:
        return pl.pallas_call(
            partial(block_kernel, dims, width, scatter),
            out_shape=jax.ShapeDtypeStruct(array.shape, array.dtype),
            grid_spec=pltpu.PrefetchScalarGridSpec(
                num_scalar_prefetch=1,
                grid=(1,),
                in_specs=[pl.BlockSpec(array.shape, lambda i, s: (0, 0))],
                out_specs=pl.BlockSpec(array.shape, lambda i, s: (0, 0)),
            ),
            cost_estimate=pl.CostEstimate(
                flops=0, bytes_accessed=4 * array.size, transcendentals=0
            ),
            name="scatter_columns" if scatter else "gather_columns",
        )(jnp.stack([row, col]).astype(jnp.int32), array)
    count = array.shape[0]
    rows, cols = n_y * n_z, n_x * n_core
    if scatter:
        split = array.reshape(count, n_core, n_x, n_y, n_z, width).transpose(0, 4, 3, 2, 1, 5)
    else:
        split = array
    split = split.reshape(count, rows, cols, width)
    split = flip_bits(flip_bits(split, 1, rows, row), 2, cols, col)
    if not scatter:
        split = split.reshape(count, n_z, n_y, n_x, n_core, width).transpose(0, 4, 3, 2, 1, 5)
    return split.reshape(array.shape)


def on_device(n_dp, n_ctx, tokens, block_order, doc_ids, w_qkv, grad_out):
    inputs = tokens[0]
    row_count, features = inputs.shape
    score_scale = 1.0 / math.sqrt(HD)
    n_core, n_x = 2, n_ctx // 2
    n_z = 4
    n_y = n_dp // n_z
    dims = (n_core, n_x, n_y, n_z)
    row, col = lax.axis_index("dp"), lax.axis_index("ctx")
    over_z = lambda a, o: exchange(a, "dp", n_dp, o * n_y)
    over_y = lambda a, o: exchange(a, "dp", n_dp, o)
    over_x = lambda a, o: exchange(a, "ctx", n_ctx, o * n_core)
    over_core = lambda a: exchange(a, "ctx", n_ctx, 1)
    near = lambda n: range(1, n)

    facts = jnp.concatenate([doc_ids[0], block_order[0]])
    facts_x = jnp.stack([facts] + [over_x(facts, o) for o in near(n_x)])
    facts_all = jnp.stack([facts_x, over_core(facts_x)]).reshape(n_ctx, -1)
    docs_all = facts_all[:, :row_count].reshape(-1)
    order_all = facts_all[:, row_count:]
    pos_all = (order_all[:, :, None] * BLOCK + jnp.arange(BLOCK, dtype=jnp.int32)).reshape(-1)
    docs_here, pos_here = docs_all[:row_count], pos_all[:row_count]

    shard = w_qkv.shape[0]
    piece = shard // n_ctx
    own = w_qkv.reshape(n_x * n_core, piece, -1)
    own = flip_bits(own, 0, n_ctx, col).reshape(n_x, n_core, piece, -1)

    def gather_yz(first):
        by_z = jnp.stack([first] + [over_z(first, o) for o in near(n_z)])
        rows = [by_z]
        for o in near(n_y):
            rows.append(jnp.concatenate([over_y(first, o)[None], over_y(by_z[1:], o)]))
        return jnp.stack(rows)

    kv_half = gather_yz(own[:, 0, :, WQ:])
    kv_half = jnp.moveaxis(kv_half, 2, 0)
    kv_half = jnp.stack([kv_half, over_core(kv_half)])
    w_kv = kv_half.reshape(features, 2 * HD)

    q_part = gather_yz(own[0, 0, :, :WQ])
    q_half = jnp.stack([q_part] + [over_x(q_part, o) for o in near(n_x)])
    q_full = jnp.stack([q_half, over_core(q_half)])
    w_q = q_full.reshape(features, WQ)

    near_inputs = reorder(inputs, dims, row, col, False)
    projected_kv = jnp.dot(near_inputs, w_kv, preferred_element_type=F32)
    cosine_table, sine_table = rope_tables(pos_here)
    key_here = rotate(projected_kv[:, :HD], cosine_table, sine_table).astype(BF16)
    value_here = projected_kv[:, HD:].astype(BF16)
    kv_here = jnp.concatenate([key_here, value_here], axis=1)
    kv_x = jnp.stack([kv_here] + [over_x(kv_here, o) for o in near(n_x)])
    kv_core = jnp.concatenate([over_core(kv_here)[None], over_core(kv_x[1:])])
    kv_all = jnp.concatenate([kv_x, kv_core]).reshape(-1, 2 * HD)
    keys, values = kv_all[:, :HD], kv_all[:, HD:]

    projected_q = jnp.dot(near_inputs, w_q, preferred_element_type=F32)
    queries = rotate(
        projected_q.reshape(row_count, HQ, HD),
        cosine_table[:, None, :],
        sine_table[:, None, :],
    ).astype(BF16)

    allowed = (docs_here[:, None] == docs_all[None, :]) & (pos_all[None, :] <= pos_here[:, None])
    allowed = allowed[:, None, :]
    scores = jnp.einsum("thd,nd->thn", queries, keys, preferred_element_type=F32) * score_scale
    row_max = jnp.max(jnp.where(allowed, scores, NEG_FILL), axis=-1)
    shifted = jnp.where(allowed, jnp.exp(scores - row_max[..., None]), 0.0)
    row_sum = jnp.sum(shifted, axis=-1)
    weighted = jnp.einsum("thn,nd->thd", shifted.astype(BF16), values, preferred_element_type=F32)
    attended = (weighted / row_sum[..., None]).astype(BF16)
    log_norm = row_max + jnp.log(row_sum)
    out_grad = grad_out[0].reshape(row_count, HQ, HD)
    row_dots = jnp.sum(out_grad.astype(F32) * attended.astype(F32), axis=-1)
    chances = jnp.where(allowed, jnp.exp(scores - log_norm[..., None]), 0.0)
    value_term = jnp.einsum(
        "thn,thd->nd", chances.astype(BF16), out_grad, preferred_element_type=F32
    )
    prob_grad = jnp.einsum("thd,nd->thn", out_grad, values, preferred_element_type=F32)
    score_grad = (chances * (prob_grad - row_dots[..., None])).astype(BF16)
    query_grad = (
        jnp.einsum("thn,nd->thd", score_grad, keys, preferred_element_type=F32) * score_scale
    )
    key_term = (
        jnp.einsum("thn,thd->nd", score_grad, queries, preferred_element_type=F32) * score_scale
    )
    kv_terms = jnp.concatenate([key_term, value_term], axis=1)
    kv_terms = kv_terms.reshape(n_core, n_x, row_count, 2 * HD)
    kv_sum = kv_terms[0] + over_core(kv_terms[1].astype(BF16)).astype(F32)
    kv_send = kv_sum[1:].astype(BF16)
    kv_mine = kv_sum[0]
    for o in near(n_x):
        kv_mine = kv_mine + over_x(kv_send[o - 1], o).astype(F32)

    q_grad = rotate(query_grad, cosine_table[:, None, :], -sine_table[:, None, :])
    q_grad = q_grad.reshape(row_count, WQ).astype(BF16)
    key_raw = rotate(kv_mine[:, :HD], cosine_table, -sine_table)
    kv_grad = jnp.concatenate([key_raw, kv_mine[:, HD:]], axis=1).astype(BF16)

    def weight_terms(columns, grad):
        return lax.dot_general(
            columns, grad, (((0,), (0,)), ((), ())), preferred_element_type=F32
        )

    half = features // 2

    def core_sum(grad):
        sent = over_core(weight_terms(near_inputs[:, half:], grad).astype(BF16))
        kept = weight_terms(near_inputs[:, :half], grad) + sent.astype(F32)
        return kept.reshape(n_x, n_y, n_z, piece, -1)

    def reduce_first(terms, over):
        total = terms[0]
        for o in near(terms.shape[0]):
            total = total + over(terms[o].astype(BF16), o).astype(F32)
        return total

    q_terms = core_sum(q_grad)
    q_terms = reduce_first(q_terms, over_x)
    q_terms = reduce_first(q_terms, over_y)
    q_terms = reduce_first(q_terms, over_z)

    kv_sums = core_sum(kv_grad)
    kv_sums = reduce_first(jnp.moveaxis(kv_sums, 0, 2), over_y)
    kv_sums = reduce_first(kv_sums, over_z)
    kv_sums = reduce_first(kv_sums, over_x)
    grad_w = jnp.concatenate([q_terms, kv_sums], axis=1)

    near_grad = (
        lax.dot_general(q_grad, w_q, (((1,), (1,)), ((), ())), preferred_element_type=F32)
        + lax.dot_general(kv_grad, w_kv, (((1,), (1,)), ((), ())), preferred_element_type=F32)
    ).astype(BF16)
    grad_inputs = reorder(near_grad, dims, row, col, True)
    return (attended.reshape(1, row_count, WQ), grad_inputs[None], grad_w)


def place_of(dims, p):
    n_core, n_x, n_y, n_z = dims
    jx, rest = p % n_x, p // n_x
    jy, rest = rest % n_y, rest // n_y
    jz, jc = rest % n_z, rest // n_z
    return (jz * n_y + jy), (jx * n_core + jc)


def vmem_call(body, out_shapes, operands, name, flops, limit=None, blocks=None, scalars=None):
    specs = []
    blocks = blocks or {}
    for i, a in enumerate(operands):
        shape, index = blocks.get(i, (a.shape, (0,) * a.ndim))
        specs.append(pl.BlockSpec(shape, lambda g, *s, index=index: index))
    size = sum(math.prod(s.block_shape) for s in specs) * 2
    size += sum(math.prod(s.shape) * 4 for s in out_shapes)
    return pl.pallas_call(
        body,
        out_shape=out_shapes,
        grid_spec=pltpu.PrefetchScalarGridSpec(
            num_scalar_prefetch=0 if scalars is None else 1,
            grid=(1,),
            in_specs=specs,
            out_specs=[
                pl.BlockSpec(s.shape, lambda g, *p, n=len(s.shape): (0,) * n) for s in out_shapes
            ],
        ),
        cost_estimate=pl.CostEstimate(flops=flops, bytes_accessed=size, transcendentals=0),
        compiler_params=pltpu.CompilerParams(vmem_limit_bytes=limit or (3 * size + (4 << 20))),
        name=name,
    )(*([] if scalars is None else [scalars]), *operands)


def shape_of(shape, dtype):
    return jax.ShapeDtypeStruct(shape, dtype)


def gather_tokens(inputs, dims, index):
    count, features = inputs.shape
    total = math.prod(dims)
    width = features // total
    n_k = dims[0] * dims[1]

    def body(index_ref, in_ref, near_ref, turned_ref, own_ref):
        row, col = index_ref[0], index_ref[1]
        for p in range(total):
            dr, dc = place_of(dims, p)
            place = (row ^ dr) * n_k + (col ^ dc)
            block = in_ref[:, pl.ds(pl.multiple_of(place * width, width), width)]
            near_ref[:, p * width : (p + 1) * width] = block
            turned_ref[p * width : (p + 1) * width, :] = block.astype(F32).T.astype(BF16)
        own_ref[...] = in_ref[:, pl.ds(pl.multiple_of(row * (n_k * width), width), n_k * width)]

    shapes = [
        shape_of((count, features), BF16),
        shape_of((features, count), BF16),
        shape_of((count, n_k * width), BF16),
    ]
    return vmem_call(body, shapes, [inputs], "gather_tokens", 0, scalars=index)


def turn(x, cos_table, sin_table):
    return x * cos_table + pltpu.roll(x, HD // 2, 1) * sin_table


def matmul(a, b, ca=1, cb=0):
    return lax.dot_general(a, b, (((ca,), (cb,)), ((), ())), preferred_element_type=F32)


def attention(first, late, near_inputs, late_places, width, kv_parts, tables, facts, out_grad):
    count = first.shape[0]
    n_parts = len(kv_parts)
    n_keys = count * sum(a.shape[0] // count for a in kv_parts)
    scale = 1.0 / math.sqrt(HD)
    n_late = len(late)

    def body(*refs):
        first_ref, near_ref = refs[:2]
        late_refs = refs[2 : 2 + n_late]
        rest = refs[2 + n_late :]
        kv_refs = rest[:n_parts]
        cos_ref, sin_ref, key_facts, here_facts, grad_ref = rest[n_parts : n_parts + 5]
        att_ref, qgrad_ref, far_ref, close_ref = rest[n_parts + 5 : n_parts + 9]
        kv_ref, kt_ref, vt_ref, bias_ref, acc_ref = rest[n_parts + 9 :]
        at = 0
        for ref in kv_refs:
            kv_ref[at : at + ref.shape[0], :] = ref[...]
            at += ref.shape[0]
        kt_ref[...] = kv_ref[:, :HD].astype(F32).T.astype(BF16)
        vt_ref[...] = kv_ref[:, HD:].astype(F32).T.astype(BF16)
        allowed = (key_facts[:, 0:1] == here_facts[0:1, :]) & (
            key_facts[:, 1:2] <= here_facts[1:2, :]
        )
        bias_ref[...] = jnp.where(allowed, 0.0, NEG_FILL)
        cos_table, sin_table = cos_ref[...], sin_ref[...]
        queries = first_ref[:, :WQ]
        for ref, places in zip(late_refs, late_places):
            for i, p in enumerate(places):
                queries = queries + matmul(near_ref[:, p * width : (p + 1) * width], ref[i])
        keys, values = kv_ref[:, :HD], kv_ref[:, HD:]
        for h in range(HQ):
            cols = slice(h * HD, (h + 1) * HD)
            q = turn(queries[:, cols], cos_table, sin_table).astype(BF16)
            grad = grad_ref[:, cols]
            scores = matmul(keys, q, 1, 1) * scale + bias_ref[...]
            top = jnp.max(scores, axis=0, keepdims=True)
            shifted = jnp.exp(scores - top)
            total = jnp.sum(shifted, axis=0, keepdims=True)
            weighted = matmul(vt_ref[...], shifted.astype(BF16))
            att = (weighted / total).astype(BF16).astype(F32)
            att_ref[:, cols] = att.T.astype(BF16)
            dots = jnp.sum(grad.astype(F32).T * att, axis=0, keepdims=True)
            chances = shifted * (1.0 / total)
            value_term = matmul(chances.astype(BF16), grad)
            prob_grad = matmul(values, grad, 1, 1)
            score_grad = (chances * (prob_grad - dots)).astype(BF16)
            key_term = matmul(score_grad, q) * scale
            if h == 0:
                acc_ref[:, :HD] = key_term
                acc_ref[:, HD:] = value_term
            else:
                acc_ref[:, :HD] += key_term
                acc_ref[:, HD:] += value_term
            q_grad = matmul(kt_ref[...], score_grad).T * scale
            qgrad_ref[:, cols] = turn(q_grad, cos_table, -sin_table).astype(BF16)
        half = n_keys // 2
        close_ref[...] = acc_ref[:half, :]
        far_ref[...] = acc_ref[half:, :].astype(BF16)

    operands = [first, near_inputs, *late, *kv_parts, *tables, *facts, out_grad]
    shapes = [
        shape_of((count, WQ), BF16),
        shape_of((count, WQ), BF16),
        shape_of((n_keys // 2, 2 * HD), BF16),
        shape_of((n_keys // 2, 2 * HD), F32),
    ]
    return pl.pallas_call(
        body,
        out_shape=shapes,
        grid=(1,),
        in_specs=[pl.BlockSpec(a.shape, lambda g, n=a.ndim: (0,) * n) for a in operands],
        out_specs=[pl.BlockSpec(s.shape, lambda g: (0, 0)) for s in shapes],
        scratch_shapes=[
            pltpu.VMEM((n_keys, 2 * HD), BF16),
            pltpu.VMEM((HD, n_keys), BF16),
            pltpu.VMEM((HD, n_keys), BF16),
            pltpu.VMEM((n_keys, count), F32),
            pltpu.VMEM((n_keys, 2 * HD), F32),
        ],
        cost_estimate=pl.CostEstimate(
            flops=14 * HQ * count * n_keys * HD,
            bytes_accessed=8 << 20,
            transcendentals=HQ * count * n_keys,
        ),
        compiler_params=pltpu.CompilerParams(vmem_limit_bytes=32 << 20),
        name="attention",
    )(*operands)


def near_device(n_dp, n_ctx, tokens, block_order, doc_ids, w_qkv, grad_out):
    inputs = tokens[0]
    count, features = inputs.shape
    n_core, n_x, n_z = 2, 2, 4
    n_y = n_dp // n_z
    dims = (n_core, n_x, n_y, n_z)
    row, col = lax.axis_index("dp"), lax.axis_index("ctx")
    index = jnp.stack([row, col]).astype(jnp.int32)
    shard = w_qkv.shape[0]
    width = shard // n_ctx
    kv_w = 2 * HD
    over_z = lambda a, o: exchange(a, "dp", n_dp, o * n_y)
    over_y = lambda a: exchange(a, "dp", n_dp, 1)
    over_x = lambda a: exchange(a, "ctx", n_ctx, n_core)
    over_core = lambda a: exchange(a, "ctx", n_ctx, 1)
    spot = lambda jc, jz, jy, jx: ((jc * n_z + jz) * n_y + jy) * n_x + jx
    cut = lambda p: slice(p * width, (p + 1) * width)

    own_rows = lax.dynamic_slice_in_dim(w_qkv, col * width, width, 0)
    other_rows = lax.dynamic_slice_in_dim(w_qkv, (col ^ n_core) * width, width, 0)
    piece = jnp.concatenate([own_rows, other_rows[:, WQ:]], axis=1)
    by_z = {o: over_z(piece, o) for o in (1, 2, 3)}
    by_y = {0: over_y(piece)}
    for o in (1, 2, 3):
        by_y[o] = over_y(by_z[o])
    main = {(0, 1): by_y[0]}
    for o in (1, 2, 3):
        main[(o, 0)] = by_z[o]
        main[(o, 1)] = by_y[o]
    groups = [[(0, 1), (1, 0)], [(1, 1), (2, 0)], [(2, 1), (3, 0)], [(3, 1)]]
    side = [over_x(jnp.stack([main[k][:, :WQ] for k in group])) for group in groups]
    mains = [{k: a for k, a in main.items()}, {k: over_core(a) for k, a in main.items()}]
    sides = [side, [over_core(a) for a in side]]

    near_inputs, turned, own_inputs = gather_tokens(inputs, dims, index)

    positions = (
        block_order[0][:, None] * BLOCK + jnp.arange(BLOCK, dtype=jnp.int32)
    ).reshape(count)
    cosine_table, sine_table = rope_tables(positions)
    cos_table = jnp.concatenate([cosine_table, cosine_table], axis=1)
    sin_table = jnp.concatenate([-sine_table, sine_table], axis=1)
    fact_rows = jnp.concatenate(
        [
            doc_ids.astype(BF16),
            jnp.repeat(block_order[0], BLOCK)[None].astype(BF16),
            jnp.zeros((14, count), BF16),
        ]
    )

    def project(start, keys, side_ids, last):
        operands, plan = [near_inputs], []
        for jc in range(n_core):
            for jz, jy in keys:
                plan.append(("main", jc, jz, jy, len(operands)))
                operands.append(mains[jc][(jz, jy)])
            for i in side_ids:
                plan.append(("side", jc, i, None, len(operands)))
                operands.append(sides[jc][i])
        n_in = len(operands)
        if start is None:
            operands += [own_inputs, w_qkv]
        else:
            operands += [start]
        if last:
            operands += [cos_table, sin_table, fact_rows]

        def body(*refs):
            near_ref = refs[0]
            if start is None:
                total = matmul(refs[n_in][...], refs[n_in + 1][...])
            else:
                total = refs[n_in][...]
            q_sum, kv_sum = total[:, :WQ], total[:, WQ:]
            for kind, jc, a, b, at in plan:
                ref = refs[at]
                if kind == "main":
                    part = matmul(near_ref[:, cut(spot(jc, a, b, 0))], ref[:, : WQ + kv_w])
                    q_sum = q_sum + part[:, :WQ]
                    kv_sum = kv_sum + part[:, WQ:]
                    kv_sum = kv_sum + matmul(
                        near_ref[:, cut(spot(jc, a, b, 1))], ref[:, WQ + kv_w :]
                    )
                else:
                    for i, (jz, jy) in enumerate(groups[a]):
                        q_sum = q_sum + matmul(near_ref[:, cut(spot(jc, jz, jy, 1))], ref[i])
            if last:
                cos_ref, sin_ref, fact_ref, out_ref, kv_ref = refs[-5:]
                out_ref[...] = q_sum
                kv_ref[:count, :HD] = turn(kv_sum[:, :HD], cos_ref[...], sin_ref[...]).astype(BF16)
                kv_ref[:count, HD:] = kv_sum[:, HD:].astype(BF16)
                kv_ref[count:, :] = fact_ref[...]
            else:
                refs[-1][:, :WQ] = q_sum
                refs[-1][:, WQ:] = kv_sum

        if last:
            shapes = [shape_of((count, WQ), F32), shape_of((count + 16, kv_w), BF16)]
        else:
            shapes = [shape_of((count, WQ + kv_w), F32)]
        flops = 2 * count * width * (WQ + 2 * kv_w) * len(plan)
        return vmem_call(body, shapes, operands, "project", flops, limit=24 << 20)

    (part,) = project(None, [(0, 1), (1, 0), (1, 1), (2, 0)], [0], False)
    q_part, kv_here = project(part, [(2, 1), (3, 0), (3, 1)], [1], True)

    kv_x = over_x(kv_here)
    kv_parts = [kv_here, kv_x, over_core(kv_here), over_core(kv_x)]
    all_facts = jnp.stack([a[count : count + 2] for a in kv_parts], axis=1).astype(jnp.int32)
    within = jnp.tile(jnp.arange(BLOCK, dtype=jnp.int32), n_ctx * count // BLOCK)
    docs_all = all_facts[0].reshape(-1)
    pos_all = all_facts[1].reshape(-1) * BLOCK + within
    key_facts = jnp.stack([docs_all, pos_all], axis=1)
    here_facts = jnp.concatenate([doc_ids, positions[None]])

    late = [sides[jc][i] for jc in range(n_core) for i in (2, 3)]
    late_places = [
        [spot(jc, jz, jy, 1) for jz, jy in groups[i]] for jc in range(n_core) for i in (2, 3)
    ]
    attended, q_grad, kv_far, kv_close = attention(
        q_part,
        late,
        near_inputs,
        late_places,
        width,
        [a[:count] for a in kv_parts],
        (cos_table, sin_table),
        (key_facts, here_facts),
        grad_out[0],
    )

    kv_got = over_core(kv_far)

    def mid_body(close_ref, got_ref, out_ref):
        out_ref[...] = (close_ref[...] + got_ref[...].astype(F32)).astype(BF16)

    (kv_send,) = vmem_call(
        mid_body,
        [shape_of((count, kv_w), BF16)],
        [kv_close, kv_got],
        "kv_pair",
        0,
        blocks={0: ((count, kv_w), (1, 0)), 1: ((count, kv_w), (1, 0))},
    )
    kv_last = over_x(kv_send)

    def kv_body(close_ref, got_ref, last_ref, cos_ref, sin_ref, out_ref):
        total = close_ref[...] + got_ref[...].astype(F32) + last_ref[...].astype(F32)
        out_ref[:, :HD] = turn(total[:, :HD], cos_ref[...], -sin_ref[...]).astype(BF16)
        out_ref[:, HD:] = total[:, HD:].astype(BF16)

    (kv_grad,) = vmem_call(
        kv_body,
        [shape_of((count, kv_w), BF16)],
        [kv_close, kv_got, kv_last, cos_table, sin_table],
        "kv_total",
        0,
        blocks={0: ((count, kv_w), (0, 0)), 1: ((count, kv_w), (0, 0))},
    )

    group_rows = n_y * n_x * width
    rows_of = lambda jy, jx: slice((jy * n_x + jx) * width, (jy * n_x + jx + 1) * width)

    def far_terms(grad, first_group, n_groups, name):
        def body(turned_ref, grad_ref, out_ref):
            out_ref[...] = matmul(turned_ref[...], grad_ref[...]).astype(BF16)

        rows = n_groups * group_rows
        return vmem_call(
            body,
            [shape_of((rows, grad.shape[1]), BF16)],
            [turned, grad],
            name,
            2 * rows * count * grad.shape[1],
            blocks={0: ((rows, count), ((n_z + first_group) // n_groups, 0))},
        )[0]

    q_core = {jz: over_core(far_terms(q_grad, jz, 1, "far_q")) for jz in (3, 2, 1, 0)}

    def x_terms(jz):
        def body(turned_ref, grad_ref, got_ref, out_ref):
            for jy in range(n_y):
                rows = rows_of(jy, 1)
                total = matmul(turned_ref[rows, :], grad_ref[...]) + got_ref[rows, :].astype(F32)
                out_ref[jy] = total.astype(BF16)

        return vmem_call(
            body,
            [shape_of((n_y, width, WQ), BF16)],
            [turned, q_grad, q_core[jz]],
            "x_terms",
            2 * n_y * width * count * WQ,
            blocks={0: ((group_rows, count), (jz, 0))},
        )[0]

    q_x = {jz: over_x(x_terms(jz)) for jz in (3, 2, 1, 0)}
    kv_core = over_core(far_terms(kv_grad, 0, n_z, "far_kv"))

    def pair_terms(jz, jy, with_q, kv_groups, added, name, dtype=BF16):
        columns = (WQ if with_q else 0) + kv_w * n_x * len(kv_groups)
        operands, blocks = [q_grad, kv_grad], {}

        def put(array, block=None):
            if block is not None:
                blocks[len(operands)] = block
            operands.append(array)
            return len(operands) - 1

        group_at = lambda g: ((group_rows, count), (g, 0))
        at_q = put(turned, group_at(jz))
        at_core = put(q_core[jz]) if with_q else None
        at_x = put(q_x[jz]) if with_q else None
        at_kv = []
        for g in kv_groups:
            a = at_q if g == jz else put(turned, group_at(g))
            at_kv.append((a, put(kv_core, ((group_rows, kv_w), (g, 0)))))
        at_add = [(put(array), source, target, size) for array, source, target, size in added]

        def body(*refs):
            out_ref = refs[-1]
            spans = []
            at = 0
            if with_q:
                total = matmul(refs[at_q][rows_of(jy, 0), :], refs[0][...])
                total = total + refs[at_core][rows_of(jy, 0), :].astype(F32)
                spans.append((0, total + refs[at_x][jy].astype(F32)))
                at = WQ
            for a, b in at_kv:
                for jx in range(n_x):
                    total = matmul(refs[a][rows_of(jy, jx), :], refs[1][...])
                    spans.append((at, total + refs[b][rows_of(jy, jx), :].astype(F32)))
                    at += kv_w
            for start, total in spans:
                size = total.shape[1]
                for i, source, target, span in at_add:
                    if target <= start and start + size <= target + span:
                        begin = source + start - target
                        total = total + refs[i][:, begin : begin + size].astype(F32)
                out_ref[:, start : start + size] = total.astype(dtype)

        return vmem_call(
            body,
            [shape_of((width, columns), dtype)],
            operands,
            name,
            2 * width * count * columns,
            blocks=blocks,
        )[0]

    wide = WQ + n_x * kv_w
    kv_wide = n_x * kv_w
    got_y = {}
    for jz in (3, 2):
        got_y[jz] = over_y(pair_terms(jz, 1, True, [jz], [], "y_terms"))
    got_y[1] = over_y(pair_terms(1, 1, True, [1, 0], [], "y_terms"))
    got_y[0] = over_y(pair_terms(0, 1, True, [], [], "y_terms"))
    got_z = {}
    for jz in (3, 2, 1):
        got_z[jz] = over_z(
            pair_terms(jz, 0, True, [jz], [(got_y[jz], 0, 0, wide)], "z_terms"), jz
        )
    kv_added = [(got_y[1], wide, 0, kv_wide)]
    kv_added += [(got_z[jz], WQ, 0, kv_wide) for jz in (3, 2, 1)]
    kv_sum = pair_terms(0, 0, False, [0], kv_added, "kv_sum", F32)
    kv_other = over_x(kv_sum[:, kv_w:].astype(BF16))
    q_added = [(got_y[0], 0, 0, WQ)] + [(got_z[jz], 0, 0, WQ) for jz in (3, 2, 1)]
    q_sum = pair_terms(0, 0, True, [], q_added, "q_sum", F32)

    def join_body(q_ref, kv_ref, other_ref, out_ref):
        out_ref[:, :WQ] = q_ref[...]
        out_ref[:, WQ:] = kv_ref[...] + other_ref[...].astype(F32)

    (grad_w,) = vmem_call(
        join_body,
        [shape_of((width, WQ + kv_w), F32)],
        [q_sum, kv_sum, kv_other],
        "join",
        0,
        blocks={1: ((width, kv_w), (0, 0))},
    )

    keys = list(main)
    operands = [q_grad, kv_grad, w_qkv]
    operands += [mains[jc][k] for jc in range(n_core) for k in keys]
    at_side = len(operands)
    operands += [sides[jc][i] for jc in range(n_core) for i in range(len(groups))]

    def input_body(index_ref, *refs):
        row, col = index_ref[0], index_ref[1]
        out_ref = refs[-1]
        grad_q, grad_kv = refs[0][...], refs[1][...]
        n_k = n_core * n_x

        def put(jc, jz, jy, jx, value):
            place = (row ^ (jz * n_y + jy)) * n_k + (col ^ (jx * n_core + jc))
            at = pl.ds(pl.multiple_of(place * width, width), width)
            out_ref[:, at] = value.astype(BF16)

        mine = matmul(grad_q, refs[2][:, :WQ], 1, 1) + matmul(grad_kv, refs[2][:, WQ:], 1, 1)
        at = pl.ds(pl.multiple_of(row * (n_k * width), width), n_k * width)
        out_ref[:, at] = mine.astype(BF16)
        for jc in range(n_core):
            for g, group in enumerate(groups):
                x_ref = refs[at_side + jc * len(groups) + g]
                for i, (jz, jy) in enumerate(group):
                    ref = refs[3 + jc * len(keys) + keys.index((jz, jy))]
                    near = matmul(grad_q, ref[:, :WQ], 1, 1)
                    near = near + matmul(grad_kv, ref[:, WQ : WQ + kv_w], 1, 1)
                    put(jc, jz, jy, 0, near)
                    far = matmul(grad_q, x_ref[i], 1, 1)
                    far = far + matmul(grad_kv, ref[:, WQ + kv_w :], 1, 1)
                    put(jc, jz, jy, 1, far)

    (grad_inputs,) = vmem_call(
        input_body,
        [shape_of((count, features), BF16)],
        operands,
        "input_grad",
        2 * count * features * (WQ + kv_w),
        limit=32 << 20,
        scalars=index,
    )
    return (attended[None], grad_inputs[None], grad_w)


def solution(mesh):
    in_specs = (
        P("dp", "ctx", None),
        P("dp", "ctx"),
        P("dp", "ctx"),
        P("dp", None),
        P("dp", "ctx", None),
    )
    out_specs = (P("dp", "ctx", None), P("dp", "ctx", None), P(("dp", "ctx"), None))
    n_dp, n_ctx = mesh.shape["dp"], mesh.shape["ctx"]
    body = near_device if (n_dp, n_ctx) == (8, 4) else on_device
    return jax.shard_map(
        partial(body, n_dp, n_ctx),
        mesh=mesh,
        in_specs=in_specs,
        out_specs=out_specs,
        check_vma=False,
    )
```

```python
import math
from functools import partial

import jax
import jax.numpy as jnp
from jax import lax
from jax.experimental import pallas as pl
from jax.experimental.pallas import tpu as pltpu
from jax.sharding import PartitionSpec as P


HQ = 4
HD = 128
BLOCK = 128
WQ = HQ * HD
ROPE_BASE = 500000.0
NEG_FILL = -1e30
BF16 = jnp.bfloat16
F32 = jnp.float32
VMEM_GRANT = 16 << 20


def rope_tables(positions):
    half = HD // 2
    inverse = 1.0 / ROPE_BASE ** (jnp.arange(half, dtype=F32) * (2.0 / HD))
    angles = positions.astype(F32)[..., None] * inverse
    return (jnp.cos(angles), jnp.sin(angles))


def rotate(values, cosine_table, sine_table):
    half = values.shape[-1] // 2
    leading = values[..., :half]
    trailing = values[..., half:]
    return jnp.concatenate(
        [
            leading * cosine_table - trailing * sine_table,
            trailing * cosine_table + leading * sine_table,
        ],
        axis=-1,
    )


def flip_bits(array, axis, size, index):
    bit = 1
    while bit < size:
        shape = array.shape
        split = array.reshape(shape[:axis] + (size // (2 * bit), 2, bit) + shape[axis + 1 :])
        array = jnp.where((index & bit) != 0, jnp.flip(split, axis + 1), split).reshape(shape)
        bit *= 2
    return array


def exchange(array, axis, size, offset):
    return lax.ppermute(array, axis, [(i, i ^ offset) for i in range(size)])


def block_kernel(dims, width, scatter, index_ref, in_ref, out_ref):
    n_core, n_x, n_y, n_z = dims
    row, col = index_ref[0], index_ref[1]
    for p in range(n_core * n_x * n_y * n_z):
        jz, rest = p % n_z, p // n_z
        jy, rest = rest % n_y, rest // n_y
        jx, jc = rest % n_x, rest // n_x
        place = (row ^ (jz * n_y + jy)) * (n_x * n_core) + (col ^ (jx * n_core + jc))
        dynamic = pl.ds(pl.multiple_of(place * width, width), width)
        static = pl.ds(p * width, width)
        if scatter:
            out_ref[:, dynamic] = in_ref[:, static]
        else:
            out_ref[:, static] = in_ref[:, dynamic]


def reorder(array, dims, row, col, scatter):
    n_core, n_x, n_y, n_z = dims
    width = array.shape[1] // (n_core * n_x * n_y * n_z)
    if width % 128 == 0:
        return pl.pallas_call(
            partial(block_kernel, dims, width, scatter),
            out_shape=jax.ShapeDtypeStruct(array.shape, array.dtype),
            grid_spec=pltpu.PrefetchScalarGridSpec(
                num_scalar_prefetch=1,
                grid=(1,),
                in_specs=[pl.BlockSpec(array.shape, lambda i, s: (0, 0))],
                out_specs=pl.BlockSpec(array.shape, lambda i, s: (0, 0)),
            ),
            cost_estimate=pl.CostEstimate(
                flops=0, bytes_accessed=4 * array.size, transcendentals=0
            ),
            name="scatter_columns" if scatter else "gather_columns",
        )(jnp.stack([row, col]).astype(jnp.int32), array)
    count = array.shape[0]
    rows, cols = n_y * n_z, n_x * n_core
    if scatter:
        split = array.reshape(count, n_core, n_x, n_y, n_z, width).transpose(0, 4, 3, 2, 1, 5)
    else:
        split = array
    split = split.reshape(count, rows, cols, width)
    split = flip_bits(flip_bits(split, 1, rows, row), 2, cols, col)
    if not scatter:
        split = split.reshape(count, n_z, n_y, n_x, n_core, width).transpose(0, 4, 3, 2, 1, 5)
    return split.reshape(array.shape)


def on_device(n_dp, n_ctx, tokens, block_order, doc_ids, w_qkv, grad_out):
    inputs = tokens[0]
    row_count, features = inputs.shape
    score_scale = 1.0 / math.sqrt(HD)
    n_core, n_x = 2, n_ctx // 2
    n_z = 4
    n_y = n_dp // n_z
    dims = (n_core, n_x, n_y, n_z)
    row, col = lax.axis_index("dp"), lax.axis_index("ctx")
    over_z = lambda a, o: exchange(a, "dp", n_dp, o * n_y)
    over_y = lambda a, o: exchange(a, "dp", n_dp, o)
    over_x = lambda a, o: exchange(a, "ctx", n_ctx, o * n_core)
    over_core = lambda a: exchange(a, "ctx", n_ctx, 1)
    near = lambda n: range(1, n)

    facts = jnp.concatenate([doc_ids[0], block_order[0]])
    facts_x = jnp.stack([facts] + [over_x(facts, o) for o in near(n_x)])
    facts_all = jnp.stack([facts_x, over_core(facts_x)]).reshape(n_ctx, -1)
    docs_all = facts_all[:, :row_count].reshape(-1)
    order_all = facts_all[:, row_count:]
    pos_all = (order_all[:, :, None] * BLOCK + jnp.arange(BLOCK, dtype=jnp.int32)).reshape(-1)
    docs_here, pos_here = docs_all[:row_count], pos_all[:row_count]

    shard = w_qkv.shape[0]
    piece = shard // n_ctx
    own = w_qkv.reshape(n_x * n_core, piece, -1)
    own = flip_bits(own, 0, n_ctx, col).reshape(n_x, n_core, piece, -1)

    def gather_yz(first):
        by_z = jnp.stack([first] + [over_z(first, o) for o in near(n_z)])
        rows = [by_z]
        for o in near(n_y):
            rows.append(jnp.concatenate([over_y(first, o)[None], over_y(by_z[1:], o)]))
        return jnp.stack(rows)

    kv_half = gather_yz(own[:, 0, :, WQ:])
    kv_half = jnp.moveaxis(kv_half, 2, 0)
    kv_half = jnp.stack([kv_half, over_core(kv_half)])
    w_kv = kv_half.reshape(features, 2 * HD)

    q_part = gather_yz(own[0, 0, :, :WQ])
    q_half = jnp.stack([q_part] + [over_x(q_part, o) for o in near(n_x)])
    q_full = jnp.stack([q_half, over_core(q_half)])
    w_q = q_full.reshape(features, WQ)

    near_inputs = reorder(inputs, dims, row, col, False)
    projected_kv = jnp.dot(near_inputs, w_kv, preferred_element_type=F32)
    cosine_table, sine_table = rope_tables(pos_here)
    key_here = rotate(projected_kv[:, :HD], cosine_table, sine_table).astype(BF16)
    value_here = projected_kv[:, HD:].astype(BF16)
    kv_here = jnp.concatenate([key_here, value_here], axis=1)
    kv_x = jnp.stack([kv_here] + [over_x(kv_here, o) for o in near(n_x)])
    kv_core = jnp.concatenate([over_core(kv_here)[None], over_core(kv_x[1:])])
    kv_all = jnp.concatenate([kv_x, kv_core]).reshape(-1, 2 * HD)
    keys, values = kv_all[:, :HD], kv_all[:, HD:]

    projected_q = jnp.dot(near_inputs, w_q, preferred_element_type=F32)
    queries = rotate(
        projected_q.reshape(row_count, HQ, HD),
        cosine_table[:, None, :],
        sine_table[:, None, :],
    ).astype(BF16)

    allowed = (docs_here[:, None] == docs_all[None, :]) & (pos_all[None, :] <= pos_here[:, None])
    allowed = allowed[:, None, :]
    scores = jnp.einsum("thd,nd->thn", queries, keys, preferred_element_type=F32) * score_scale
    row_max = jnp.max(jnp.where(allowed, scores, NEG_FILL), axis=-1)
    shifted = jnp.where(allowed, jnp.exp(scores - row_max[..., None]), 0.0)
    row_sum = jnp.sum(shifted, axis=-1)
    weighted = jnp.einsum("thn,nd->thd", shifted.astype(BF16), values, preferred_element_type=F32)
    attended = (weighted / row_sum[..., None]).astype(BF16)
    log_norm = row_max + jnp.log(row_sum)
    out_grad = grad_out[0].reshape(row_count, HQ, HD)
    row_dots = jnp.sum(out_grad.astype(F32) * attended.astype(F32), axis=-1)
    chances = jnp.where(allowed, jnp.exp(scores - log_norm[..., None]), 0.0)
    value_term = jnp.einsum(
        "thn,thd->nd", chances.astype(BF16), out_grad, preferred_element_type=F32
    )
    prob_grad = jnp.einsum("thd,nd->thn", out_grad, values, preferred_element_type=F32)
    score_grad = (chances * (prob_grad - row_dots[..., None])).astype(BF16)
    query_grad = (
        jnp.einsum("thn,nd->thd", score_grad, keys, preferred_element_type=F32) * score_scale
    )
    key_term = (
        jnp.einsum("thn,thd->nd", score_grad, queries, preferred_element_type=F32) * score_scale
    )
    kv_terms = jnp.concatenate([key_term, value_term], axis=1)
    kv_terms = kv_terms.reshape(n_core, n_x, row_count, 2 * HD)
    kv_sum = kv_terms[0] + over_core(kv_terms[1].astype(BF16)).astype(F32)
    kv_send = kv_sum[1:].astype(BF16)
    kv_mine = kv_sum[0]
    for o in near(n_x):
        kv_mine = kv_mine + over_x(kv_send[o - 1], o).astype(F32)

    q_grad = rotate(query_grad, cosine_table[:, None, :], -sine_table[:, None, :])
    q_grad = q_grad.reshape(row_count, WQ).astype(BF16)
    key_raw = rotate(kv_mine[:, :HD], cosine_table, -sine_table)
    kv_grad = jnp.concatenate([key_raw, kv_mine[:, HD:]], axis=1).astype(BF16)

    def weight_terms(columns, grad):
        return lax.dot_general(
            columns, grad, (((0,), (0,)), ((), ())), preferred_element_type=F32
        )

    half = features // 2

    def core_sum(grad):
        sent = over_core(weight_terms(near_inputs[:, half:], grad).astype(BF16))
        kept = weight_terms(near_inputs[:, :half], grad) + sent.astype(F32)
        return kept.reshape(n_x, n_y, n_z, piece, -1)

    def reduce_first(terms, over):
        total = terms[0]
        for o in near(terms.shape[0]):
            total = total + over(terms[o].astype(BF16), o).astype(F32)
        return total

    q_terms = core_sum(q_grad)
    q_terms = reduce_first(q_terms, over_x)
    q_terms = reduce_first(q_terms, over_y)
    q_terms = reduce_first(q_terms, over_z)

    kv_sums = core_sum(kv_grad)
    kv_sums = reduce_first(jnp.moveaxis(kv_sums, 0, 2), over_y)
    kv_sums = reduce_first(kv_sums, over_z)
    kv_sums = reduce_first(kv_sums, over_x)
    grad_w = jnp.concatenate([q_terms, kv_sums], axis=1)

    near_grad = (
        lax.dot_general(q_grad, w_q, (((1,), (1,)), ((), ())), preferred_element_type=F32)
        + lax.dot_general(kv_grad, w_kv, (((1,), (1,)), ((), ())), preferred_element_type=F32)
    ).astype(BF16)
    grad_inputs = reorder(near_grad, dims, row, col, True)
    return (attended.reshape(1, row_count, WQ), grad_inputs[None], grad_w)


def place_of(dims, p):
    n_core, n_x, n_y, n_z = dims
    jx, rest = p % n_x, p // n_x
    jy, rest = rest % n_y, rest // n_y
    jz, jc = rest % n_z, rest // n_z
    return (jz * n_y + jy), (jx * n_core + jc)


def vmem_call(body, out_shapes, operands, flops, blocks=None, scalars=None, scratch=()):
    blocks = blocks or {}
    count = len(operands)
    lead = 0 if scalars is None else 1

    def cut_body(*refs):
        refs = list(refs)
        for i, (start, size) in blocks.items():
            refs[lead + i] = refs[lead + i].at[pl.ds(start, size)]
        body(*refs)

    sizes = [math.prod(a.shape) * a.dtype.itemsize for a in operands]
    sizes += [math.prod(s.shape) * s.dtype.itemsize for s in out_shapes]
    whole = pl.BlockSpec(memory_space=pltpu.VMEM)
    return pl.pallas_call(
        cut_body,
        out_shape=out_shapes,
        in_specs=[pl.BlockSpec(memory_space=pltpu.SMEM)] * lead + [whole] * count,
        out_specs=[whole] * len(out_shapes),
        scratch_shapes=scratch,
        cost_estimate=pl.CostEstimate(flops=flops, bytes_accessed=sum(sizes), transcendentals=0),
        compiler_params=pltpu.CompilerParams(vmem_limit_bytes=VMEM_GRANT),
    )(*([] if scalars is None else [scalars]), *operands)


def shape_of(shape, dtype):
    return jax.ShapeDtypeStruct(shape, dtype)


def gather_tokens(inputs, dims, index):
    count, features = inputs.shape
    total = math.prod(dims)
    width = features // total
    n_k = dims[0] * dims[1]

    def body(index_ref, in_ref, near_ref, turned_ref, own_ref):
        row, col = index_ref[0], index_ref[1]
        for p in range(total):
            dr, dc = place_of(dims, p)
            place = (row ^ dr) * n_k + (col ^ dc)
            block = in_ref[:, pl.ds(pl.multiple_of(place * width, width), width)]
            near_ref[:, p * width : (p + 1) * width] = block
            turned_ref[p * width : (p + 1) * width, :] = block.astype(F32).T.astype(BF16)
        own_ref[...] = in_ref[:, pl.ds(pl.multiple_of(row * (n_k * width), width), n_k * width)]

    shapes = [
        shape_of((count, features), BF16),
        shape_of((features, count), BF16),
        shape_of((count, n_k * width), BF16),
    ]
    return vmem_call(body, shapes, [inputs], 0, scalars=index)


def turn(x, cos_table, sin_table):
    return x * cos_table + pltpu.roll(x, HD // 2, 1) * sin_table


def matmul(a, b, ca=1, cb=0):
    return lax.dot_general(a, b, (((ca,), (cb,)), ((), ())), preferred_element_type=F32)


def attention(first, late, near_inputs, late_places, width, kv_parts, tables, out_grad):
    count = first.shape[0]
    n_parts = len(kv_parts)
    n_keys = count * n_parts
    scale = 1.0 / math.sqrt(HD)
    n_late = len(late)

    def body(*refs):
        first_ref, near_ref = refs[:2]
        late_refs = refs[2 : 2 + n_late]
        rest = refs[2 + n_late :]
        kv_refs = rest[:n_parts]
        cos_ref, sin_ref, grad_ref = rest[n_parts : n_parts + 3]
        att_ref, qgrad_ref, far_ref, close_ref = rest[n_parts + 3 : n_parts + 7]
        kv_ref, kt_ref, vt_ref, bias_ref, acc_ref = rest[n_parts + 7 :]
        here = kv_refs[0][count:, :].astype(F32)
        within = lax.broadcasted_iota(jnp.int32, (1, count), 1) % BLOCK
        here_docs, here_pos = here[0:1], here[1:2] * BLOCK + within.astype(F32)
        within = lax.broadcasted_iota(jnp.int32, (count, 1), 0) % BLOCK
        for i, ref in enumerate(kv_refs):
            rows = slice(i * count, (i + 1) * count)
            kv_ref[rows, :] = ref[:count, :]
            there = ref[count:, :].astype(F32).T
            pos = there[:, 1:2] * BLOCK + within.astype(F32)
            allowed = (there[:, 0:1] == here_docs) & (pos <= here_pos)
            bias_ref[rows, :] = jnp.where(allowed, 0.0, NEG_FILL)
        kt_ref[...] = kv_ref[:, :HD].astype(F32).T.astype(BF16)
        vt_ref[...] = kv_ref[:, HD:].astype(F32).T.astype(BF16)
        cos_table, sin_table = cos_ref[...], sin_ref[...]
        queries = first_ref[:, :WQ]
        for ref, places in zip(late_refs, late_places):
            for i, p in enumerate(places):
                queries = queries + matmul(near_ref[:, p * width : (p + 1) * width], ref[i])
        keys, values = kv_ref[:, :HD], kv_ref[:, HD:]
        for h in range(HQ):
            cols = slice(h * HD, (h + 1) * HD)
            q = turn(queries[:, cols], cos_table, sin_table).astype(BF16)
            grad = grad_ref[:, cols]
            scores = matmul(keys, q, 1, 1) * scale + bias_ref[...]
            top = jnp.max(scores, axis=0, keepdims=True)
            shifted = jnp.exp(scores - top)
            total = jnp.sum(shifted, axis=0, keepdims=True)
            weighted = matmul(vt_ref[...], shifted.astype(BF16))
            att = (weighted / total).astype(BF16).astype(F32)
            att_ref[:, cols] = att.T.astype(BF16)
            dots = jnp.sum(grad.astype(F32).T * att, axis=0, keepdims=True)
            chances = shifted * (1.0 / total)
            value_term = matmul(chances.astype(BF16), grad)
            prob_grad = matmul(values, grad, 1, 1)
            score_grad = (chances * (prob_grad - dots)).astype(BF16)
            key_term = matmul(score_grad, q) * scale
            if h == 0:
                acc_ref[:, :HD] = key_term
                acc_ref[:, HD:] = value_term
            else:
                acc_ref[:, :HD] += key_term
                acc_ref[:, HD:] += value_term
            q_grad = matmul(kt_ref[...], score_grad).T * scale
            qgrad_ref[:, cols] = turn(q_grad, cos_table, -sin_table).astype(BF16)
        half = n_keys // 2
        close_ref[...] = acc_ref[:half, :]
        far_ref[...] = acc_ref[half:, :].astype(BF16)

    operands = [first, near_inputs, *late, *kv_parts, *tables, out_grad]
    shapes = [
        shape_of((count, WQ), BF16),
        shape_of((count, WQ), BF16),
        shape_of((n_keys // 2, 2 * HD), BF16),
        shape_of((n_keys // 2, 2 * HD), F32),
    ]
    return vmem_call(
        body,
        shapes,
        operands,
        14 * HQ * count * n_keys * HD,
        scratch=[
            pltpu.VMEM((n_keys, 2 * HD), BF16),
            pltpu.VMEM((HD, n_keys), BF16),
            pltpu.VMEM((HD, n_keys), BF16),
            pltpu.VMEM((n_keys, count), F32),
            pltpu.VMEM((n_keys, 2 * HD), F32),
        ],
    )


def near_device(n_dp, n_ctx, *args):
    return near_body(n_dp, n_ctx, *args)


def near_body(n_dp, n_ctx, tokens, block_order, doc_ids, w_qkv, grad_out):
    inputs = tokens[0]
    count, features = inputs.shape
    n_core, n_x, n_z = 2, 2, 4
    n_y = n_dp // n_z
    dims = (n_core, n_x, n_y, n_z)
    index = jnp.stack([lax.axis_index("dp"), lax.axis_index("ctx")]).astype(jnp.int32)
    index = lax.optimization_barrier(index)
    col = index[1]
    shard = w_qkv.shape[0]
    width = shard // n_ctx
    kv_w = 2 * HD

    over_z = lambda a, o: exchange(a, "dp", n_dp, o * n_y)
    over_y = lambda a: exchange(a, "dp", n_dp, 1)
    over_x = lambda a: exchange(a, "ctx", n_ctx, n_core)
    over_core = lambda a: exchange(a, "ctx", n_ctx, 1)
    spot = lambda jc, jz, jy, jx: ((jc * n_z + jz) * n_y + jy) * n_x + jx
    cut = lambda p: slice(p * width, (p + 1) * width)

    own_rows = lax.dynamic_slice_in_dim(w_qkv, col * width, width, 0)
    other_rows = lax.dynamic_slice_in_dim(w_qkv, (col ^ n_core) * width, width, 0)
    piece = jnp.concatenate([own_rows, other_rows[:, WQ:]], axis=1)
    by_z = {o: over_z(piece, o) for o in (1, 2, 3)}
    by_y = {0: over_y(piece)}
    for o in (1, 2, 3):
        by_y[o] = over_y(by_z[o])
    main = {(0, 1): by_y[0]}
    for o in (1, 2, 3):
        main[(o, 0)] = by_z[o]
        main[(o, 1)] = by_y[o]
    groups = [[(0, 1), (1, 0)], [(1, 1), (2, 0)], [(2, 1), (3, 0)], [(3, 1)]]
    side = [over_x(jnp.stack([main[k][:, :WQ] for k in group])) for group in groups]
    mains = [main, {k: over_core(a) for k, a in main.items()}]
    sides = [side, [over_core(a) for a in side]]

    near_inputs, turned, own_inputs = gather_tokens(inputs, dims, index)

    positions = (
        block_order[0][:, None] * BLOCK + jnp.arange(BLOCK, dtype=jnp.int32)
    ).reshape(count)
    cosine_table, sine_table = rope_tables(positions)
    cos_table = jnp.concatenate([cosine_table, cosine_table], axis=1)
    sin_table = jnp.concatenate([-sine_table, sine_table], axis=1)
    fact_rows = jnp.concatenate(
        [
            doc_ids.astype(BF16),
            jnp.repeat(block_order[0], BLOCK)[None].astype(BF16),
            jnp.zeros((14, count), BF16),
        ]
    )

    def project(start, keys, side_ids, last):
        operands, plan = [near_inputs], []
        for jc in range(n_core):
            for jz, jy in keys:
                plan.append(("main", jc, jz, jy, len(operands)))
                operands.append(mains[jc][(jz, jy)])
            for i in side_ids:
                plan.append(("side", jc, i, None, len(operands)))
                operands.append(sides[jc][i])
        n_in = len(operands)
        if start is None:
            operands += [own_inputs, w_qkv]
        else:
            operands += [start]
        if last:
            operands += [cos_table, sin_table, fact_rows]

        def body(*refs):
            near_ref = refs[0]
            if start is None:
                total = matmul(refs[n_in][...], refs[n_in + 1][...])
            else:
                total = refs[n_in][...]
            q_sum, kv_sum = total[:, :WQ], total[:, WQ:]
            for kind, jc, a, b, at in plan:
                ref = refs[at]
                if kind == "main":
                    part = matmul(near_ref[:, cut(spot(jc, a, b, 0))], ref[:, : WQ + kv_w])
                    q_sum = q_sum + part[:, :WQ]
                    kv_sum = kv_sum + part[:, WQ:]
                    kv_sum = kv_sum + matmul(
                        near_ref[:, cut(spot(jc, a, b, 1))], ref[:, WQ + kv_w :]
                    )
                else:
                    for i, (jz, jy) in enumerate(groups[a]):
                        q_sum = q_sum + matmul(near_ref[:, cut(spot(jc, jz, jy, 1))], ref[i])
            if last:
                cos_ref, sin_ref, fact_ref, out_ref, kv_ref = refs[-5:]
                out_ref[...] = q_sum
                kv_ref[:count, :HD] = turn(kv_sum[:, :HD], cos_ref[...], sin_ref[...]).astype(BF16)
                kv_ref[:count, HD:] = kv_sum[:, HD:].astype(BF16)
                kv_ref[count:, :] = fact_ref[...]
            else:
                refs[-1][:, :WQ] = q_sum
                refs[-1][:, WQ:] = kv_sum

        if last:
            shapes = [shape_of((count, WQ), F32), shape_of((count + 16, kv_w), BF16)]
        else:
            shapes = [shape_of((count, WQ + kv_w), F32)]
        flops = 2 * count * width * (WQ + 2 * kv_w) * len(plan)
        return vmem_call(body, shapes, operands, flops)

    (part,) = project(None, [(0, 1), (1, 0), (1, 1), (2, 0), (2, 1), (3, 0)], [0, 1], False)
    q_part, kv_here = project(part, [(3, 1)], [], True)

    kv_x = over_x(kv_here)
    kv_parts = [kv_here, kv_x, over_core(kv_here), over_core(kv_x)]
    late = [sides[jc][i] for jc in range(n_core) for i in (2, 3)]
    late_places = [
        [spot(jc, jz, jy, 1) for jz, jy in groups[i]] for jc in range(n_core) for i in (2, 3)
    ]
    attended, q_grad, kv_far, kv_close = attention(
        q_part,
        late,
        near_inputs,
        late_places,
        width,
        kv_parts,
        (cos_table, sin_table),
        grad_out[0],
    )

    kv_got = over_core(kv_far)

    def mid_body(close_ref, got_ref, out_ref):
        out_ref[...] = (close_ref[...] + got_ref[...].astype(F32)).astype(BF16)

    (kv_send,) = vmem_call(
        mid_body,
        [shape_of((count, kv_w), BF16)],
        [kv_close, kv_got],
        0,
        blocks={0: (count, count), 1: (count, count)},
    )
    kv_last = over_x(kv_send)

    def kv_body(close_ref, got_ref, last_ref, cos_ref, sin_ref, out_ref):
        total = close_ref[...] + got_ref[...].astype(F32) + last_ref[...].astype(F32)
        out_ref[:, :HD] = turn(total[:, :HD], cos_ref[...], -sin_ref[...]).astype(BF16)
        out_ref[:, HD:] = total[:, HD:].astype(BF16)

    (kv_grad,) = vmem_call(
        kv_body,
        [shape_of((count, kv_w), BF16)],
        [kv_close, kv_got, kv_last, cos_table, sin_table],
        0,
        blocks={0: (0, count), 1: (0, count)},
    )

    group_rows = n_y * n_x * width
    rows_of = lambda jy, jx: slice((jy * n_x + jx) * width, (jy * n_x + jx + 1) * width)

    def far_terms(grad, first_group, n_groups):
        def body(turned_ref, grad_ref, out_ref):
            out_ref[...] = matmul(turned_ref[...], grad_ref[...]).astype(BF16)

        rows = n_groups * group_rows
        return vmem_call(
            body,
            [shape_of((rows, grad.shape[1]), BF16)],
            [turned, grad],
            2 * rows * count * grad.shape[1],
            blocks={0: ((n_z + first_group) * group_rows, rows)},
        )[0]

    q_core = {jz: over_core(far_terms(q_grad, jz, 1)) for jz in (3, 2, 1, 0)}

    def x_terms(jz):
        def body(turned_ref, grad_ref, got_ref, out_ref):
            for jy in range(n_y):
                rows = rows_of(jy, 1)
                total = matmul(turned_ref[rows, :], grad_ref[...]) + got_ref[rows, :].astype(F32)
                out_ref[jy] = total.astype(BF16)

        return vmem_call(
            body,
            [shape_of((n_y, width, WQ), BF16)],
            [turned, q_grad, q_core[jz]],
            2 * n_y * width * count * WQ,
            blocks={0: (jz * group_rows, group_rows)},
        )[0]

    q_x = {jz: over_x(x_terms(jz)) for jz in (3, 2, 1, 0)}
    kv_core = over_core(far_terms(kv_grad, 0, n_z))

    def q_terms(jz, jy, added, dtype=BF16):
        def body(turned_ref, grad_ref, core_ref, x_ref, *refs):
            rows = rows_of(jy, 0)
            total = matmul(turned_ref[rows, :], grad_ref[...]) + core_ref[rows, :].astype(F32)
            total = total + x_ref[jy].astype(F32)
            for ref in refs[:-1]:
                total = total + ref[...].astype(F32)
            refs[-1][...] = total.astype(dtype)

        return vmem_call(
            body,
            [shape_of((width, WQ), dtype)],
            [turned, q_grad, q_core[jz], q_x[jz], *added],
            2 * width * count * WQ,
            blocks={0: (jz * group_rows, group_rows)},
        )[0]

    kv_wide = n_x * kv_w

    def kv_terms(z_list, jy, added, dtype=BF16):
        def body(turned_ref, grad_ref, core_ref, *refs):
            out_ref = refs[-1]
            for i, jz in enumerate(z_list):
                for jx in range(n_x):
                    at = (jz * n_y * n_x + jy * n_x + jx) * width
                    rows, cols = slice(at, at + width), slice(jx * kv_w, (jx + 1) * kv_w)
                    total = matmul(turned_ref[rows, :], grad_ref[...])
                    total = total + core_ref[rows, :].astype(F32)
                    for ref, (_, start) in zip(refs[:-1], added):
                        here = slice(start + i * width, start + (i + 1) * width)
                        total = total + ref[here, cols].astype(F32)
                    out_ref[i * width : (i + 1) * width, cols] = total.astype(dtype)

        return vmem_call(
            body,
            [shape_of((len(z_list) * width, kv_wide), dtype)],
            [turned, kv_grad, kv_core, *[array for array, _ in added]],
            2 * len(z_list) * width * count * kv_wide,
        )[0]

    kv_y = over_y(kv_terms(range(n_z), 1, []))
    q_y = {jz: over_y(q_terms(jz, 1, [])) for jz in (3, 2, 1, 0)}
    kv_z = {jz: over_z(kv_terms([jz], 0, [(kv_y, jz * width)]), jz) for jz in (3, 2, 1)}
    q_z = {jz: over_z(q_terms(jz, 0, [q_y[jz]]), jz) for jz in (3, 2, 1)}
    kv_sum = kv_terms([0], 0, [(kv_y, 0)] + [(a, 0) for a in kv_z.values()], F32)
    kv_other = over_x(kv_sum[:, kv_w:].astype(BF16))

    def sum_body(turned_ref, grad_ref, core_ref, x_ref, *refs):
        kv_ref, other_ref, out_ref = refs[-3:]
        rows = rows_of(0, 0)
        total = matmul(turned_ref[rows, :], grad_ref[...]) + core_ref[rows, :].astype(F32)
        total = total + x_ref[0].astype(F32)
        for ref in refs[:-3]:
            total = total + ref[...].astype(F32)
        out_ref[:, :WQ] = total
        out_ref[:, WQ:] = kv_ref[:, :kv_w] + other_ref[...].astype(F32)

    (grad_w,) = vmem_call(
        sum_body,
        [shape_of((width, WQ + kv_w), F32)],
        [turned, q_grad, q_core[0], q_x[0], q_y[0], *q_z.values(), kv_sum, kv_other],
        2 * width * count * WQ,
        blocks={0: (0, group_rows)},
    )

    keys = list(main)
    operands = [q_grad, kv_grad, w_qkv]
    operands += [mains[jc][k] for jc in range(n_core) for k in keys]
    at_side = len(operands)
    operands += [sides[jc][i] for jc in range(n_core) for i in range(len(groups))]

    def input_body(index_ref, *refs):
        row, col = index_ref[0], index_ref[1]
        out_ref = refs[-1]
        grad_q, grad_kv = refs[0][...], refs[1][...]
        n_k = n_core * n_x

        def put(jc, jz, jy, jx, value):
            place = (row ^ (jz * n_y + jy)) * n_k + (col ^ (jx * n_core + jc))
            at = pl.ds(pl.multiple_of(place * width, width), width)
            out_ref[:, at] = value.astype(BF16)

        mine = matmul(grad_q, refs[2][:, :WQ], 1, 1) + matmul(grad_kv, refs[2][:, WQ:], 1, 1)
        at = pl.ds(pl.multiple_of(row * (n_k * width), width), n_k * width)
        out_ref[:, at] = mine.astype(BF16)
        for jc in range(n_core):
            for g, group in enumerate(groups):
                x_ref = refs[at_side + jc * len(groups) + g]
                for i, (jz, jy) in enumerate(group):
                    ref = refs[3 + jc * len(keys) + keys.index((jz, jy))]
                    near = matmul(grad_q, ref[:, :WQ], 1, 1)
                    near = near + matmul(grad_kv, ref[:, WQ : WQ + kv_w], 1, 1)
                    put(jc, jz, jy, 0, near)
                    far = matmul(grad_q, x_ref[i], 1, 1)
                    far = far + matmul(grad_kv, ref[:, WQ + kv_w :], 1, 1)
                    put(jc, jz, jy, 1, far)

    (grad_inputs,) = vmem_call(
        input_body,
        [shape_of((count, features), BF16)],
        operands,
        2 * count * features * (WQ + kv_w),
        scalars=index,
    )
    return (attended[None], grad_inputs[None], grad_w)


def solution(mesh):
    in_specs = (
        P("dp", "ctx", None),
        P("dp", "ctx"),
        P("dp", "ctx"),
        P("dp", None),
        P("dp", "ctx", None),
    )
    out_specs = (P("dp", "ctx", None), P("dp", "ctx", None), P(("dp", "ctx"), None))
    n_dp, n_ctx = mesh.shape["dp"], mesh.shape["ctx"]
    near = (n_dp, n_ctx) == (8, 4)
    body = near_device if near else on_device
    return jax.shard_map(
        partial(body, n_dp, n_ctx),
        mesh=mesh,
        in_specs=in_specs,
        out_specs=out_specs,
        check_vma=False,
    )
```

```python
import math
from functools import partial

import jax
import jax.numpy as jnp
from jax import lax
from jax.experimental import pallas as pl
from jax.experimental.pallas import tpu as pltpu
from jax.sharding import PartitionSpec as P


HQ = 4
HD = 128
BLOCK = 128
WQ = HQ * HD
ROPE_BASE = 500000.0
NEG_FILL = -1e30
BF16 = jnp.bfloat16
F32 = jnp.float32
VMEM_GRANT = 16 << 20


def rope_tables(positions):
    half = HD // 2
    inverse = 1.0 / ROPE_BASE ** (jnp.arange(half, dtype=F32) * (2.0 / HD))
    angles = positions.astype(F32)[..., None] * inverse
    return (jnp.cos(angles), jnp.sin(angles))


def rotate(values, cosine_table, sine_table):
    half = values.shape[-1] // 2
    leading = values[..., :half]
    trailing = values[..., half:]
    return jnp.concatenate(
        [
            leading * cosine_table - trailing * sine_table,
            trailing * cosine_table + leading * sine_table,
        ],
        axis=-1,
    )


def flip_bits(array, axis, size, index):
    bit = 1
    while bit < size:
        shape = array.shape
        split = array.reshape(shape[:axis] + (size // (2 * bit), 2, bit) + shape[axis + 1 :])
        array = jnp.where((index & bit) != 0, jnp.flip(split, axis + 1), split).reshape(shape)
        bit *= 2
    return array


def exchange(array, axis, size, offset):
    return lax.ppermute(array, axis, [(i, i ^ offset) for i in range(size)])


def block_kernel(dims, width, scatter, index_ref, in_ref, out_ref):
    n_core, n_x, n_y, n_z = dims
    row, col = index_ref[0], index_ref[1]
    for p in range(n_core * n_x * n_y * n_z):
        jz, rest = p % n_z, p // n_z
        jy, rest = rest % n_y, rest // n_y
        jx, jc = rest % n_x, rest // n_x
        place = (row ^ (jz * n_y + jy)) * (n_x * n_core) + (col ^ (jx * n_core + jc))
        dynamic = pl.ds(pl.multiple_of(place * width, width), width)
        static = pl.ds(p * width, width)
        if scatter:
            out_ref[:, dynamic] = in_ref[:, static]
        else:
            out_ref[:, static] = in_ref[:, dynamic]


def reorder(array, dims, row, col, scatter):
    n_core, n_x, n_y, n_z = dims
    width = array.shape[1] // (n_core * n_x * n_y * n_z)
    if width % 128 == 0:
        return pl.pallas_call(
            partial(block_kernel, dims, width, scatter),
            out_shape=jax.ShapeDtypeStruct(array.shape, array.dtype),
            grid_spec=pltpu.PrefetchScalarGridSpec(
                num_scalar_prefetch=1,
                grid=(1,),
                in_specs=[pl.BlockSpec(array.shape, lambda i, s: (0, 0))],
                out_specs=pl.BlockSpec(array.shape, lambda i, s: (0, 0)),
            ),
            cost_estimate=pl.CostEstimate(
                flops=0, bytes_accessed=4 * array.size, transcendentals=0
            ),
            name="scatter_columns" if scatter else "gather_columns",
        )(jnp.stack([row, col]).astype(jnp.int32), array)
    count = array.shape[0]
    rows, cols = n_y * n_z, n_x * n_core
    if scatter:
        split = array.reshape(count, n_core, n_x, n_y, n_z, width).transpose(0, 4, 3, 2, 1, 5)
    else:
        split = array
    split = split.reshape(count, rows, cols, width)
    split = flip_bits(flip_bits(split, 1, rows, row), 2, cols, col)
    if not scatter:
        split = split.reshape(count, n_z, n_y, n_x, n_core, width).transpose(0, 4, 3, 2, 1, 5)
    return split.reshape(array.shape)


def on_device(n_dp, n_ctx, tokens, block_order, doc_ids, w_qkv, grad_out):
    inputs = tokens[0]
    row_count, features = inputs.shape
    score_scale = 1.0 / math.sqrt(HD)
    n_core, n_x = 2, n_ctx // 2
    n_z = 4
    n_y = n_dp // n_z
    dims = (n_core, n_x, n_y, n_z)
    row, col = lax.axis_index("dp"), lax.axis_index("ctx")
    over_z = lambda a, o: exchange(a, "dp", n_dp, o * n_y)
    over_y = lambda a, o: exchange(a, "dp", n_dp, o)
    over_x = lambda a, o: exchange(a, "ctx", n_ctx, o * n_core)
    over_core = lambda a: exchange(a, "ctx", n_ctx, 1)
    near = lambda n: range(1, n)

    facts = jnp.concatenate([doc_ids[0], block_order[0]])
    facts_x = jnp.stack([facts] + [over_x(facts, o) for o in near(n_x)])
    facts_all = jnp.stack([facts_x, over_core(facts_x)]).reshape(n_ctx, -1)
    docs_all = facts_all[:, :row_count].reshape(-1)
    order_all = facts_all[:, row_count:]
    pos_all = (order_all[:, :, None] * BLOCK + jnp.arange(BLOCK, dtype=jnp.int32)).reshape(-1)
    docs_here, pos_here = docs_all[:row_count], pos_all[:row_count]

    shard = w_qkv.shape[0]
    piece = shard // n_ctx
    own = w_qkv.reshape(n_x * n_core, piece, -1)
    own = flip_bits(own, 0, n_ctx, col).reshape(n_x, n_core, piece, -1)

    def gather_yz(first):
        by_z = jnp.stack([first] + [over_z(first, o) for o in near(n_z)])
        rows = [by_z]
        for o in near(n_y):
            rows.append(jnp.concatenate([over_y(first, o)[None], over_y(by_z[1:], o)]))
        return jnp.stack(rows)

    kv_half = gather_yz(own[:, 0, :, WQ:])
    kv_half = jnp.moveaxis(kv_half, 2, 0)
    kv_half = jnp.stack([kv_half, over_core(kv_half)])
    w_kv = kv_half.reshape(features, 2 * HD)

    q_part = gather_yz(own[0, 0, :, :WQ])
    q_half = jnp.stack([q_part] + [over_x(q_part, o) for o in near(n_x)])
    q_full = jnp.stack([q_half, over_core(q_half)])
    w_q = q_full.reshape(features, WQ)

    near_inputs = reorder(inputs, dims, row, col, False)
    projected_kv = jnp.dot(near_inputs, w_kv, preferred_element_type=F32)
    cosine_table, sine_table = rope_tables(pos_here)
    key_here = rotate(projected_kv[:, :HD], cosine_table, sine_table).astype(BF16)
    value_here = projected_kv[:, HD:].astype(BF16)
    kv_here = jnp.concatenate([key_here, value_here], axis=1)
    kv_x = jnp.stack([kv_here] + [over_x(kv_here, o) for o in near(n_x)])
    kv_core = jnp.concatenate([over_core(kv_here)[None], over_core(kv_x[1:])])
    kv_all = jnp.concatenate([kv_x, kv_core]).reshape(-1, 2 * HD)
    keys, values = kv_all[:, :HD], kv_all[:, HD:]

    projected_q = jnp.dot(near_inputs, w_q, preferred_element_type=F32)
    queries = rotate(
        projected_q.reshape(row_count, HQ, HD),
        cosine_table[:, None, :],
        sine_table[:, None, :],
    ).astype(BF16)

    allowed = (docs_here[:, None] == docs_all[None, :]) & (pos_all[None, :] <= pos_here[:, None])
    allowed = allowed[:, None, :]
    scores = jnp.einsum("thd,nd->thn", queries, keys, preferred_element_type=F32) * score_scale
    row_max = jnp.max(jnp.where(allowed, scores, NEG_FILL), axis=-1)
    shifted = jnp.where(allowed, jnp.exp(scores - row_max[..., None]), 0.0)
    row_sum = jnp.sum(shifted, axis=-1)
    weighted = jnp.einsum("thn,nd->thd", shifted.astype(BF16), values, preferred_element_type=F32)
    attended = (weighted / row_sum[..., None]).astype(BF16)
    log_norm = row_max + jnp.log(row_sum)
    out_grad = grad_out[0].reshape(row_count, HQ, HD)
    row_dots = jnp.sum(out_grad.astype(F32) * attended.astype(F32), axis=-1)
    chances = jnp.where(allowed, jnp.exp(scores - log_norm[..., None]), 0.0)
    value_term = jnp.einsum(
        "thn,thd->nd", chances.astype(BF16), out_grad, preferred_element_type=F32
    )
    prob_grad = jnp.einsum("thd,nd->thn", out_grad, values, preferred_element_type=F32)
    score_grad = (chances * (prob_grad - row_dots[..., None])).astype(BF16)
    query_grad = (
        jnp.einsum("thn,nd->thd", score_grad, keys, preferred_element_type=F32) * score_scale
    )
    key_term = (
        jnp.einsum("thn,thd->nd", score_grad, queries, preferred_element_type=F32) * score_scale
    )
    kv_terms = jnp.concatenate([key_term, value_term], axis=1)
    kv_terms = kv_terms.reshape(n_core, n_x, row_count, 2 * HD)
    kv_sum = kv_terms[0] + over_core(kv_terms[1].astype(BF16)).astype(F32)
    kv_send = kv_sum[1:].astype(BF16)
    kv_mine = kv_sum[0]
    for o in near(n_x):
        kv_mine = kv_mine + over_x(kv_send[o - 1], o).astype(F32)

    q_grad = rotate(query_grad, cosine_table[:, None, :], -sine_table[:, None, :])
    q_grad = q_grad.reshape(row_count, WQ).astype(BF16)
    key_raw = rotate(kv_mine[:, :HD], cosine_table, -sine_table)
    kv_grad = jnp.concatenate([key_raw, kv_mine[:, HD:]], axis=1).astype(BF16)

    def weight_terms(columns, grad):
        return lax.dot_general(
            columns, grad, (((0,), (0,)), ((), ())), preferred_element_type=F32
        )

    half = features // 2

    def core_sum(grad):
        sent = over_core(weight_terms(near_inputs[:, half:], grad).astype(BF16))
        kept = weight_terms(near_inputs[:, :half], grad) + sent.astype(F32)
        return kept.reshape(n_x, n_y, n_z, piece, -1)

    def reduce_first(terms, over):
        total = terms[0]
        for o in near(terms.shape[0]):
            total = total + over(terms[o].astype(BF16), o).astype(F32)
        return total

    q_terms = core_sum(q_grad)
    q_terms = reduce_first(q_terms, over_x)
    q_terms = reduce_first(q_terms, over_y)
    q_terms = reduce_first(q_terms, over_z)

    kv_sums = core_sum(kv_grad)
    kv_sums = reduce_first(jnp.moveaxis(kv_sums, 0, 2), over_y)
    kv_sums = reduce_first(kv_sums, over_z)
    kv_sums = reduce_first(kv_sums, over_x)
    grad_w = jnp.concatenate([q_terms, kv_sums], axis=1)

    near_grad = (
        lax.dot_general(q_grad, w_q, (((1,), (1,)), ((), ())), preferred_element_type=F32)
        + lax.dot_general(kv_grad, w_kv, (((1,), (1,)), ((), ())), preferred_element_type=F32)
    ).astype(BF16)
    grad_inputs = reorder(near_grad, dims, row, col, True)
    return (attended.reshape(1, row_count, WQ), grad_inputs[None], grad_w)


def place_of(dims, p):
    n_core, n_x, n_y, n_z = dims
    jx, rest = p % n_x, p // n_x
    jy, rest = rest % n_y, rest // n_y
    jz, jc = rest % n_z, rest // n_z
    return (jz * n_y + jy), (jx * n_core + jc)


def vmem_call(body, out_shapes, operands, flops, blocks=None, scalars=None, scratch=()):
    blocks = blocks or {}
    count = len(operands)
    lead = 0 if scalars is None else 1

    def cut_body(*refs):
        refs = list(refs)
        for i, (start, size) in blocks.items():
            refs[lead + i] = refs[lead + i].at[pl.ds(start, size)]
        body(*refs)

    sizes = [math.prod(a.shape) * a.dtype.itemsize for a in operands]
    sizes += [math.prod(s.shape) * s.dtype.itemsize for s in out_shapes]
    whole = pl.BlockSpec(memory_space=pltpu.VMEM)
    return pl.pallas_call(
        cut_body,
        out_shape=out_shapes,
        in_specs=[pl.BlockSpec(memory_space=pltpu.SMEM)] * lead + [whole] * count,
        out_specs=[whole] * len(out_shapes),
        scratch_shapes=scratch,
        cost_estimate=pl.CostEstimate(flops=flops, bytes_accessed=sum(sizes), transcendentals=0),
        compiler_params=pltpu.CompilerParams(vmem_limit_bytes=VMEM_GRANT),
    )(*([] if scalars is None else [scalars]), *operands)


def shape_of(shape, dtype):
    return jax.ShapeDtypeStruct(shape, dtype)


def gather_tokens(inputs, dims, index):
    count, features = inputs.shape
    total = math.prod(dims)
    width = features // total
    n_k = dims[0] * dims[1]

    def body(index_ref, in_ref, near_ref, turned_ref, own_ref):
        row, col = index_ref[0], index_ref[1]
        for p in range(total):
            dr, dc = place_of(dims, p)
            place = (row ^ dr) * n_k + (col ^ dc)
            block = in_ref[:, pl.ds(pl.multiple_of(place * width, width), width)]
            near_ref[:, p * width : (p + 1) * width] = block
            turned_ref[p * width : (p + 1) * width, :] = block.astype(F32).T.astype(BF16)
        own_ref[...] = in_ref[:, pl.ds(pl.multiple_of(row * (n_k * width), width), n_k * width)]

    shapes = [
        shape_of((count, features), BF16),
        shape_of((features, count), BF16),
        shape_of((count, n_k * width), BF16),
    ]
    return vmem_call(body, shapes, [inputs], 0, scalars=index)


def turn(x, cos_table, sin_table):
    return x * cos_table + pltpu.roll(x, HD // 2, 1) * sin_table


def matmul(a, b, ca=1, cb=0):
    return lax.dot_general(a, b, (((ca,), (cb,)), ((), ())), preferred_element_type=F32)


def attention(first, late, near_inputs, late_places, width, kv_parts, tables, out_grad):
    count = first.shape[0]
    n_parts = len(kv_parts)
    n_keys = count * n_parts
    scale = 1.0 / math.sqrt(HD)
    n_late = len(late)

    def body(*refs):
        first_ref, near_ref = refs[:2]
        late_refs = refs[2 : 2 + n_late]
        rest = refs[2 + n_late :]
        kv_refs = rest[:n_parts]
        cos_ref, sin_ref, grad_ref = rest[n_parts : n_parts + 3]
        att_ref, qgrad_ref, far_ref, close_ref = rest[n_parts + 3 : n_parts + 7]
        kv_ref, kt_ref, vt_ref, bias_ref, acc_ref = rest[n_parts + 7 :]
        here = kv_refs[0][count:, :].astype(F32)
        within = lax.broadcasted_iota(jnp.int32, (1, count), 1) % BLOCK
        here_docs, here_pos = here[0:1], here[1:2] * BLOCK + within.astype(F32)
        within = lax.broadcasted_iota(jnp.int32, (count, 1), 0) % BLOCK
        for i, ref in enumerate(kv_refs):
            rows = slice(i * count, (i + 1) * count)
            kv_ref[rows, :] = ref[:count, :]
            there = ref[count:, :].astype(F32).T
            pos = there[:, 1:2] * BLOCK + within.astype(F32)
            allowed = (there[:, 0:1] == here_docs) & (pos <= here_pos)
            bias_ref[rows, :] = jnp.where(allowed, 0.0, NEG_FILL)
        kt_ref[...] = kv_ref[:, :HD].astype(F32).T.astype(BF16)
        vt_ref[...] = kv_ref[:, HD:].astype(F32).T.astype(BF16)
        cos_table, sin_table = cos_ref[...], sin_ref[...]
        queries = first_ref[:, :WQ]
        for ref, places in zip(late_refs, late_places):
            for i, p in enumerate(places):
                queries = queries + matmul(near_ref[:, p * width : (p + 1) * width], ref[i])
        keys, values = kv_ref[:, :HD], kv_ref[:, HD:]
        for h in range(HQ):
            cols = slice(h * HD, (h + 1) * HD)
            q = turn(queries[:, cols], cos_table, sin_table).astype(BF16)
            grad = grad_ref[:, cols]
            scores = matmul(keys, q, 1, 1) * scale + bias_ref[...]
            top = jnp.max(scores, axis=0, keepdims=True)
            shifted = jnp.exp(scores - top)
            total = jnp.sum(shifted, axis=0, keepdims=True)
            weighted = matmul(vt_ref[...], shifted.astype(BF16))
            att = (weighted / total).astype(BF16).astype(F32)
            att_ref[:, cols] = att.T.astype(BF16)
            dots = jnp.sum(grad.astype(F32).T * att, axis=0, keepdims=True)
            chances = shifted * (1.0 / total)
            value_term = matmul(chances.astype(BF16), grad)
            prob_grad = matmul(values, grad, 1, 1)
            score_grad = (chances * (prob_grad - dots)).astype(BF16)
            key_term = matmul(score_grad, q) * scale
            if h == 0:
                acc_ref[:, :HD] = key_term
                acc_ref[:, HD:] = value_term
            else:
                acc_ref[:, :HD] += key_term
                acc_ref[:, HD:] += value_term
            q_grad = matmul(kt_ref[...], score_grad).T * scale
            qgrad_ref[:, cols] = turn(q_grad, cos_table, -sin_table).astype(BF16)
        half = n_keys // 2
        close_ref[...] = acc_ref[:half, :]
        far_ref[...] = acc_ref[half:, :].astype(BF16)

    operands = [first, near_inputs, *late, *kv_parts, *tables, out_grad]
    shapes = [
        shape_of((count, WQ), BF16),
        shape_of((count, WQ), BF16),
        shape_of((n_keys // 2, 2 * HD), BF16),
        shape_of((n_keys // 2, 2 * HD), F32),
    ]
    return vmem_call(
        body,
        shapes,
        operands,
        14 * HQ * count * n_keys * HD,
        scratch=[
            pltpu.VMEM((n_keys, 2 * HD), BF16),
            pltpu.VMEM((HD, n_keys), BF16),
            pltpu.VMEM((HD, n_keys), BF16),
            pltpu.VMEM((n_keys, count), F32),
            pltpu.VMEM((n_keys, 2 * HD), F32),
        ],
    )


def near_device(n_dp, n_ctx, *args):
    return near_body(n_dp, n_ctx, *args)


def near_body(n_dp, n_ctx, tokens, block_order, doc_ids, w_qkv, grad_out):
    inputs = tokens[0]
    count, features = inputs.shape
    n_core, n_x, n_z = 2, 2, 4
    n_y = n_dp // n_z
    dims = (n_core, n_x, n_y, n_z)
    row, col = lax.optimization_barrier(
        (lax.axis_index("dp").astype(jnp.int32), lax.axis_index("ctx").astype(jnp.int32))
    )
    index = jnp.stack([row, col])
    shard = w_qkv.shape[0]
    width = shard // n_ctx
    kv_w = 2 * HD

    over_z = lambda a, o: exchange(a, "dp", n_dp, o * n_y)
    over_y = lambda a: exchange(a, "dp", n_dp, 1)
    over_x = lambda a: exchange(a, "ctx", n_ctx, n_core)
    over_core = lambda a: exchange(a, "ctx", n_ctx, 1)
    spot = lambda jc, jz, jy, jx: ((jc * n_z + jz) * n_y + jy) * n_x + jx
    cut = lambda p: slice(p * width, (p + 1) * width)

    own_rows = lax.dynamic_slice_in_dim(w_qkv, col * width, width, 0)
    other_rows = lax.dynamic_slice_in_dim(w_qkv, (col ^ n_core) * width, width, 0)
    piece = jnp.concatenate([own_rows, other_rows[:, WQ:]], axis=1)
    by_z = {o: over_z(piece, o) for o in (1, 2)}
    by_z[3] = over_z(by_z[2], 1)
    by_y = {0: over_y(piece)}
    for o in (1, 2, 3):
        by_y[o] = over_y(by_z[o])
    main = {(0, 1): by_y[0]}
    for o in (1, 2, 3):
        main[(o, 0)] = by_z[o]
        main[(o, 1)] = by_y[o]
    groups = [[(0, 1), (1, 0)], [(1, 1), (2, 0)], [(2, 1), (3, 0)], [(3, 1)]]

    def pack(arrays):
        def body(*refs):
            for j, ref in enumerate(refs[:-1]):
                refs[-1][j] = ref[:, :WQ]

        return vmem_call(body, [shape_of((len(arrays), width, WQ), BF16)], arrays, 0)[0]

    side = [over_x(pack([main[k] for k in group])) for group in groups]
    mains = [main, {k: over_core(a) for k, a in main.items()}]
    sides = [side, [over_core(a) for a in side]]

    near_inputs, turned, own_inputs = gather_tokens(inputs, dims, index)

    positions = (
        block_order[0][:, None] * BLOCK + jnp.arange(BLOCK, dtype=jnp.int32)
    ).reshape(count)
    cosine_table, sine_table = rope_tables(positions)
    cos_table = jnp.concatenate([cosine_table, cosine_table], axis=1)
    sin_table = jnp.concatenate([-sine_table, sine_table], axis=1)
    fact_rows = jnp.concatenate(
        [
            doc_ids.astype(BF16),
            jnp.repeat(block_order[0], BLOCK)[None].astype(BF16),
            jnp.zeros((14, count), BF16),
        ]
    )

    def project(start, keys, side_ids, last):
        operands, plan = [near_inputs], []
        for jc in range(n_core):
            for jz, jy in keys:
                plan.append(("main", jc, jz, jy, len(operands)))
                operands.append(mains[jc][(jz, jy)])
            for i in side_ids:
                plan.append(("side", jc, i, None, len(operands)))
                operands.append(sides[jc][i])
        n_in = len(operands)
        if start is None:
            operands += [own_inputs, w_qkv]
        else:
            operands += [start]
        if last:
            operands += [cos_table, sin_table, fact_rows]

        def body(*refs):
            near_ref = refs[0]
            if start is None:
                total = matmul(refs[n_in][...], refs[n_in + 1][...])
            else:
                total = refs[n_in][...]
            q_sum, kv_sum = total[:, :WQ], total[:, WQ:]
            for kind, jc, a, b, at in plan:
                ref = refs[at]
                if kind == "main":
                    part = matmul(near_ref[:, cut(spot(jc, a, b, 0))], ref[:, : WQ + kv_w])
                    q_sum = q_sum + part[:, :WQ]
                    kv_sum = kv_sum + part[:, WQ:]
                    kv_sum = kv_sum + matmul(
                        near_ref[:, cut(spot(jc, a, b, 1))], ref[:, WQ + kv_w :]
                    )
                else:
                    for i, (jz, jy) in enumerate(groups[a]):
                        q_sum = q_sum + matmul(near_ref[:, cut(spot(jc, jz, jy, 1))], ref[i])
            if last:
                cos_ref, sin_ref, fact_ref, out_ref, kv_ref = refs[-5:]
                out_ref[...] = q_sum
                kv_ref[:count, :HD] = turn(kv_sum[:, :HD], cos_ref[...], sin_ref[...]).astype(BF16)
                kv_ref[:count, HD:] = kv_sum[:, HD:].astype(BF16)
                kv_ref[count:, :] = fact_ref[...]
            else:
                refs[-1][:, :WQ] = q_sum
                refs[-1][:, WQ:] = kv_sum

        if last:
            shapes = [shape_of((count, WQ), F32), shape_of((count + 16, kv_w), BF16)]
        else:
            shapes = [shape_of((count, WQ + kv_w), F32)]
        flops = 2 * count * width * (WQ + 2 * kv_w) * len(plan)
        return vmem_call(body, shapes, operands, flops)

    (part,) = project(None, [(0, 1), (1, 0), (1, 1), (2, 0), (2, 1), (3, 0)], [0, 1], False)
    q_part, kv_here = project(part, [(3, 1)], [], True)

    kv_x = over_x(kv_here)
    kv_parts = [kv_here, kv_x, over_core(kv_here), over_core(kv_x)]
    late = [sides[jc][i] for jc in range(n_core) for i in (2, 3)]
    late_places = [
        [spot(jc, jz, jy, 1) for jz, jy in groups[i]] for jc in range(n_core) for i in (2, 3)
    ]
    attended, q_grad, kv_far, kv_close = attention(
        q_part,
        late,
        near_inputs,
        late_places,
        width,
        kv_parts,
        (cos_table, sin_table),
        grad_out[0],
    )

    kv_got = over_core(kv_far)

    def mid_body(close_ref, got_ref, out_ref):
        out_ref[...] = (close_ref[...] + got_ref[...].astype(F32)).astype(BF16)

    (kv_send,) = vmem_call(
        mid_body,
        [shape_of((count, kv_w), BF16)],
        [kv_close, kv_got],
        0,
        blocks={0: (count, count), 1: (count, count)},
    )
    kv_last = over_x(kv_send)

    def kv_body(close_ref, got_ref, last_ref, cos_ref, sin_ref, out_ref):
        total = close_ref[...] + got_ref[...].astype(F32) + last_ref[...].astype(F32)
        out_ref[:, :HD] = turn(total[:, :HD], cos_ref[...], -sin_ref[...]).astype(BF16)
        out_ref[:, HD:] = total[:, HD:].astype(BF16)

    (kv_grad,) = vmem_call(
        kv_body,
        [shape_of((count, kv_w), BF16)],
        [kv_close, kv_got, kv_last, cos_table, sin_table],
        0,
        blocks={0: (0, count), 1: (0, count)},
    )

    group_rows = n_y * n_x * width
    rows_of = lambda jy, jx: slice((jy * n_x + jx) * width, (jy * n_x + jx + 1) * width)

    def far_terms(grad, first_group, n_groups):
        def body(turned_ref, grad_ref, out_ref):
            out_ref[...] = matmul(turned_ref[...], grad_ref[...]).astype(BF16)

        rows = n_groups * group_rows
        return vmem_call(
            body,
            [shape_of((rows, grad.shape[1]), BF16)],
            [turned, grad],
            2 * rows * count * grad.shape[1],
            blocks={0: ((n_z + first_group) * group_rows, rows)},
        )[0]

    q_core = {jz: over_core(far_terms(q_grad, jz, 1)) for jz in (3, 1, 2, 0)}

    def x_terms(jz):
        def body(turned_ref, grad_ref, got_ref, out_ref):
            for jy in range(n_y):
                rows = rows_of(jy, 1)
                total = matmul(turned_ref[rows, :], grad_ref[...]) + got_ref[rows, :].astype(F32)
                out_ref[jy] = total.astype(BF16)

        return vmem_call(
            body,
            [shape_of((n_y, width, WQ), BF16)],
            [turned, q_grad, q_core[jz]],
            2 * n_y * width * count * WQ,
            blocks={0: (jz * group_rows, group_rows)},
        )[0]

    q_x = {jz: over_x(x_terms(jz)) for jz in (3, 1, 2, 0)}
    kv_core = over_core(far_terms(kv_grad, 0, n_z))

    def q_terms(z_list, jy, added):
        n_z_list = len(z_list)

        def body(turned_ref, grad_ref, *refs):
            core_refs, x_refs = refs[:n_z_list], refs[n_z_list : 2 * n_z_list]
            for i, jz in enumerate(z_list):
                rows = rows_of(jy, 0)
                at = jz * group_rows + rows.start
                total = matmul(turned_ref[at : at + width, :], grad_ref[...])
                total = total + core_refs[i][rows, :].astype(F32) + x_refs[i][jy].astype(F32)
                for ref, (_, pick, start) in zip(refs[2 * n_z_list : -1], added):
                    if pick == jz:
                        total = total + ref[start : start + width, :].astype(F32)
                refs[-1][i * width : (i + 1) * width, :] = total.astype(BF16)

        operands = [turned, q_grad] + [q_core[jz] for jz in z_list] + [q_x[jz] for jz in z_list]
        return vmem_call(
            body,
            [shape_of((n_z_list * width, WQ), BF16)],
            operands + [array for array, _, _ in added],
            2 * n_z_list * width * count * WQ,
        )[0]

    kv_wide = n_x * kv_w

    def kv_terms(z_list, jy, added, dtype=BF16):
        def body(turned_ref, grad_ref, core_ref, *refs):
            out_ref = refs[-1]
            for i, jz in enumerate(z_list):
                for jx in range(n_x):
                    at = (jz * n_y * n_x + jy * n_x + jx) * width
                    rows, cols = slice(at, at + width), slice(jx * kv_w, (jx + 1) * kv_w)
                    total = matmul(turned_ref[rows, :], grad_ref[...])
                    total = total + core_ref[rows, :].astype(F32)
                    for ref, (_, start) in zip(refs[:-1], added):
                        here = slice(start + i * width, start + (i + 1) * width)
                        total = total + ref[here, cols].astype(F32)
                    out_ref[i * width : (i + 1) * width, cols] = total.astype(dtype)

        return vmem_call(
            body,
            [shape_of((len(z_list) * width, kv_wide), dtype)],
            [turned, kv_grad, kv_core, *[array for array, _ in added]],
            2 * len(z_list) * width * count * kv_wide,
        )[0]

    kv_y31 = over_y(kv_terms([3, 1], 1, []))
    kv_y20 = over_y(kv_terms([2, 0], 1, []))
    q_y = {jz: over_y(q_terms([jz], 1, [])) for jz in (3, 1, 2, 0)}
    kv_z31 = over_z(kv_terms([3, 1], 0, [(kv_y31, 0)]), 1)
    kv_z2 = over_z(kv_terms([2], 0, [(kv_y20, 0), (kv_z31, 0)]), 2)
    q_z31 = q_terms([3, 1], 0, [(q_y[3], 3, 0), (q_y[1], 1, 0)])
    q_z31 = over_z(q_z31, 1)
    q_z2 = q_terms([2], 0, [(q_y[2], 2, 0), (q_z31, 2, 0)])
    q_z2 = over_z(q_z2, 2)
    kv_sum = kv_terms([0], 0, [(kv_y20, width), (kv_z31, width), (kv_z2, 0)], F32)
    kv_other = over_x(kv_sum[:, kv_w:].astype(BF16))

    def sum_body(turned_ref, grad_ref, core_ref, x_ref, y_ref, z_ref, z2_ref, *refs):
        kv_ref, other_ref, out_ref = refs
        rows = rows_of(0, 0)
        total = matmul(turned_ref[rows, :], grad_ref[...]) + core_ref[rows, :].astype(F32)
        total = total + x_ref[0].astype(F32)
        total = total + y_ref[...].astype(F32) + z_ref[width:, :].astype(F32)
        out_ref[:, :WQ] = total + z2_ref[...].astype(F32)
        out_ref[:, WQ:] = kv_ref[:, :kv_w] + other_ref[...].astype(F32)

    (grad_w,) = vmem_call(
        sum_body,
        [shape_of((width, WQ + kv_w), F32)],
        [turned, q_grad, q_core[0], q_x[0], q_y[0], q_z31, q_z2, kv_sum, kv_other],
        2 * width * count * WQ,
        blocks={0: (0, group_rows)},
    )

    keys = list(main)
    operands = [q_grad, kv_grad, w_qkv]
    operands += [mains[jc][k] for jc in range(n_core) for k in keys]
    at_side = len(operands)
    operands += [sides[jc][i] for jc in range(n_core) for i in range(len(groups))]

    def input_body(index_ref, *refs):
        row, col = index_ref[0], index_ref[1]
        out_ref = refs[-1]
        grad_q, grad_kv = refs[0][...], refs[1][...]
        n_k = n_core * n_x

        def put(jc, jz, jy, jx, value):
            place = (row ^ (jz * n_y + jy)) * n_k + (col ^ (jx * n_core + jc))
            at = pl.ds(pl.multiple_of(place * width, width), width)
            out_ref[:, at] = value.astype(BF16)

        mine = matmul(grad_q, refs[2][:, :WQ], 1, 1) + matmul(grad_kv, refs[2][:, WQ:], 1, 1)
        at = pl.ds(pl.multiple_of(row * (n_k * width), width), n_k * width)
        out_ref[:, at] = mine.astype(BF16)
        for jc in range(n_core):
            for g, group in enumerate(groups):
                x_ref = refs[at_side + jc * len(groups) + g]
                for i, (jz, jy) in enumerate(group):
                    ref = refs[3 + jc * len(keys) + keys.index((jz, jy))]
                    near = matmul(grad_q, ref[:, :WQ], 1, 1)
                    near = near + matmul(grad_kv, ref[:, WQ : WQ + kv_w], 1, 1)
                    put(jc, jz, jy, 0, near)
                    far = matmul(grad_q, x_ref[i], 1, 1)
                    far = far + matmul(grad_kv, ref[:, WQ + kv_w :], 1, 1)
                    put(jc, jz, jy, 1, far)

    (grad_inputs,) = vmem_call(
        input_body,
        [shape_of((count, features), BF16)],
        operands,
        2 * count * features * (WQ + kv_w),
        scalars=index,
    )
    return (attended[None], grad_inputs[None], grad_w)


def solution(mesh):
    in_specs = (
        P("dp", "ctx", None),
        P("dp", "ctx"),
        P("dp", "ctx"),
        P("dp", None),
        P("dp", "ctx", None),
    )
    out_specs = (P("dp", "ctx", None), P("dp", "ctx", None), P(("dp", "ctx"), None))
    n_dp, n_ctx = mesh.shape["dp"], mesh.shape["ctx"]
    near = (n_dp, n_ctx) == (8, 4)
    body = near_device if near else on_device
    return jax.shard_map(
        partial(body, n_dp, n_ctx),
        mesh=mesh,
        in_specs=in_specs,
        out_specs=out_specs,
        check_vma=False,
    )
```
